32 devices in a mesh: dp: 8 (over y, x, core), fsdp: 4 (over z).
Axes of the slice: x: 2, y: 2, z: 4, core: 2. Of those that a mesh axis runs over, the one named last changes fastest.
Arguments:
- gradients: bfloat16 [8, 512, 8192], P('dp', None, 'fsdp'), may hold values from -1.5 to 1.5
- momentum: float32 [512, 8192], P('dp', 'fsdp'), may hold values from -1500 to 1500
- weight: float32 [512, 8192], P(None, 'fsdp'), may hold values from -3 to 3
- logit_peaks: int32 [32, 32], P(('dp', 'fsdp')), may hold values from 0 to 479, as said below
- clip_threshold: int32 [1], replicated, may hold values from 60 to 120
Outputs:
- new_weight: float32 [512, 8192], P(None, 'fsdp')
- new_momentum: float32 [512, 8192], P('dp', 'fsdp')
- update_norm: float32 [1], replicated
The draws below stay inside these ranges and needn't reach their ends.
Inputs may be any that keep to these rules, and one draw needn't show every extreme that they name: `logit_peaks`: for every head, the largest entry over all rows is at least 40.
All inputs are finite; a program needn't handle non-finite values.
Results may differ from the reference program's by a relative error of at most 0.0023.
Values may be sent and summed in bfloat16 or wider, within the bound.
A program may use at most 64 MiB of HBM per device.

```python
import math
import jax
import jax.numpy as jnp
from jax import lax

KVL = 512
NOPE = 128
VDIM = 128
HEADS = 32
ITERS = 3
KVO = 8192
N_DP = 8
N_FSDP = 4


def draw_logit_peaks(key, part):
    first, second, third, fourth = jax.random.split(key, 4)
    device_count = N_DP * N_FSDP
    head_index = jnp.arange(HEADS)
    ceilings = jax.random.randint(first, (HEADS,), 40, 480)
    shuffled = jax.random.permutation(second, HEADS)
    ceilings = jnp.where(head_index == shuffled[0], 479, jnp.where(head_index == shuffled[1], 40, ceilings))
    holders = jax.random.randint(third, (HEADS,), 0, device_count)
    lesser = jax.random.randint(fourth, (device_count, HEADS), 0, 1048576) % (ceilings // 3 + 1)[None, :]
    row_index = jnp.arange(device_count)[:, None]
    return jnp.where(row_index == holders[None, :], ceilings[None, :], lesser).astype(jnp.int32)


def draw_momentum(key, part):
    first = jax.random.fold_in(key, 0)
    third = jax.random.fold_in(key, 2)
    noise = jax.random.truncated_normal(first, -4.0, 4.0, (KVL, KVO), jnp.float32)
    row_pos = jnp.arange(KVL, dtype=jnp.float32) / (KVL - 1)
    row_scale = jnp.exp(row_pos * 2.302585)[:, None]
    block_cols = KVO // (N_FSDP * N_DP)
    col_index = jnp.arange(KVO)
    block_index = col_index % (KVO // N_FSDP) // block_cols
    block_levels = jnp.exp(jax.random.uniform(third, (N_DP,), jnp.float32) * 2.0794415)
    block_scale = block_levels[block_index][None, :]
    values = row_scale * block_scale * noise
    return values.astype(jnp.float32)


def raised(entries, stream_key, source, target, shards_of, factor):
    owner, partner = [(jnp.arange(entries.shape[position]) // (entries.shape[position] // shards_of)).reshape([-1 if axis == position else 1 for axis in range(entries.ndim)]) for position in (source, target)]
    chosen = jax.random.permutation(stream_key, shards_of)[partner]
    strong = (owner == chosen) | (owner == (partner + shards_of // 2) % shards_of)
    return jnp.where(strong, factor * entries, entries)


def level_of(own_key, shape, pieces, least, high):
    def one(axis_at, shards_of):
        steps = jax.random.uniform(jax.random.fold_in(jax.random.fold_in(own_key, 6), axis_at), (shards_of,), jnp.float32, least / len(pieces), high / len(pieces))
        return jnp.repeat(jnp.exp(steps), shape[axis_at] // shards_of).reshape((-1,) + (1,) * (len(shape) - axis_at - 1))

    factor_of = one(*pieces[0])
    for cut in pieces[1:]:
        factor_of = factor_of * one(*cut)
    return factor_of


def bell_draw(own_key, shape, spread, limit, cuts=(), held_as=jnp.bfloat16):
    factor_of = level_of(own_key, shape, cuts, -0.22, 0.18) if cuts else 1.0
    result = jax.random.normal(own_key, shape, jnp.float32) * spread * factor_of
    return jnp.minimum(jnp.maximum(result, -limit), limit).astype(held_as)


def bell_draw_with(key, dims, deviation, most, cuts, heavy, kind=jnp.bfloat16):
    result = deviation * jax.random.normal(key, dims, jnp.float32)
    if cuts:
        result = result * level_of(key, dims, cuts, -0.22, 0.18)
    return jnp.clip(raised(result, jax.random.fold_in(key, 3), *heavy), -most, most).astype(kind)


def setup_inputs(seed: int = 0) -> dict:
    streams_of = jax.random.split(jax.random.key(seed), 6)
    gradients = bell_draw_with(streams_of[0], (N_DP, KVL, KVO), 0.25, 1.5, ((0, 8), (2, 4)), (0, 1, 8, 2.0))
    momentum = draw_momentum(jax.random.fold_in(streams_of[5], 71), 0)
    weight = bell_draw(streams_of[2], (KVL, KVO), 0.5, 3.0, ((1, 4),), jnp.float32)
    logit_peaks = draw_logit_peaks(jax.random.fold_in(streams_of[5], 71), 0)
    clip_threshold = jax.random.randint(streams_of[4], (1,), 60, 121).astype(jnp.int32)
    return {"gradients": gradients, "momentum": momentum, "weight": weight, "logit_peaks": logit_peaks, "clip_threshold": clip_threshold}


quintic_terms = (3.4445, -4.775, 2.0315)
learning_rate = 0.5
weight_decay = 0.1
momentum_decay = 0.95
update_gain = 0.2
epsilon = 1e-07

def column_factors(global_peaks, clip_threshold):
    largest = lax.optimization_barrier(jnp.max(global_peaks, axis=0)).astype(jnp.float32)
    clip_ratio = jnp.minimum(1.0, clip_threshold.astype(jnp.float32)[0] / largest)
    key_scale = jnp.sqrt(clip_ratio)
    per_head = jnp.concatenate([jnp.broadcast_to(key_scale[:, None], (HEADS, NOPE)), jnp.ones((HEADS, VDIM), jnp.float32)], axis=1)
    return per_head.reshape(HEADS * (NOPE + VDIM))

def orthogonalize(matrix):
    current = matrix
    for iteration in range(ITERS):
        square = lax.dot_general(current, current, (((1,), (1,)), ((), ())), precision=lax.Precision.HIGHEST, preferred_element_type=jnp.float32)
        combined = quintic_terms[1] * square + quintic_terms[2] * jnp.dot(square, square, precision=lax.Precision.HIGHEST, preferred_element_type=jnp.float32)
        current = quintic_terms[0] * current + jnp.dot(combined, current, precision=lax.Precision.HIGHEST, preferred_element_type=jnp.float32)
    return current

def reference(gradients, momentum, weight, logit_peaks, clip_threshold):
    summed = lax.optimization_barrier(jnp.sum(gradients.astype(jnp.float32), axis=0))
    new_momentum = momentum_decay * momentum + summed
    blended = summed + momentum_decay * new_momentum
    square_total = jnp.sum(blended * blended)
    update_norm = jnp.sqrt(square_total / (KVL * KVO)).reshape(1).astype(jnp.float32)
    normalized = blended / (jnp.sqrt(square_total) + epsilon)
    orthogonal = orthogonalize(normalized)
    update_scale = update_gain * math.sqrt(max(KVL, KVO))
    stepped = weight - learning_rate * (update_scale * orthogonal + weight_decay * weight)
    new_weight = stepped * column_factors(logit_peaks, clip_threshold)[None, :]
    return (new_weight, new_momentum, update_norm)
```

```python
import functools
import math

import jax
import jax.numpy as jnp
from jax import lax
from jax.experimental import pallas as pl
from jax.experimental.pallas import tpu as pltpu
from jax.sharding import PartitionSpec as P

KVL = 512
NOPE = 128
VDIM = 128
HEADS = 32
ITERS = 3
KVO = 8192


quintic_terms = (3.4445, -4.775, 2.0315)
learning_rate = 0.5
weight_decay = 0.1
momentum_decay = 0.95
update_gain = 0.2
epsilon = 1e-07

STEP = 16
MESH = pl.DeviceIdType.MESH
f32 = jnp.float32
bf16 = jnp.bfloat16


def exchange(
    dp_count,
    fsdp_count,
    grad_all,
    momentum_all,
    peaks_all,
    new_momentum,
    columns,
    gram,
    stats_out,
    kept,
    pair,
    momentum,
    peaks,
    out_first,
    in_first,
    out_second,
    in_second,
    gram_own,
    gram_in,
    stats_in,
    stats_wide,
    local_sem,
    pair_sem,
    first_sem,
    second_sem,
    gather_sem,
    relay_sem,
    core_sem,
    gram_wide_sem,
    gram_sem,
    stats_sem,
    stats_wide_sem,
):
    d = lax.axis_index("dp")
    f = lax.axis_index("fsdp")
    chips = dp_count // 2
    q = d // 2
    core = d % 2
    steps = kept.shape[1]
    width = momentum.shape[1]
    half = width // 2
    left = pl.ds(0, half)
    right = pl.ds(half, half)
    square_plane = chips == 4
    partner = (2 * q + 1 - core, f)

    barrier = pltpu.get_barrier_semaphore()
    for k in range(1, dp_count):
        pl.semaphore_signal(
            barrier, inc=1, device_id=(lax.rem(d + k, dp_count), f), device_id_type=MESH
        )
    for k in range(1, fsdp_count):
        pl.semaphore_signal(
            barrier, inc=1, device_id=(d, lax.rem(f + k, fsdp_count)), device_id_type=MESH
        )
    kept_copy = pltpu.make_async_copy(grad_all.at[:, core], kept, local_sem.at[0])
    momentum_copy = pltpu.make_async_copy(momentum_all, momentum, local_sem.at[1])
    peaks_copy = pltpu.make_async_copy(peaks_all, peaks, local_sem.at[2])
    kept_copy.start()
    momentum_copy.start()
    peaks_copy.start()
    pl.semaphore_wait(barrier, dp_count + fsdp_count - 2)

    started = []

    def send(source, target, sems, where, device):
        copy = pltpu.make_async_remote_copy(
            src_ref=source,
            dst_ref=target,
            send_sem=sems.at[(0,) + where],
            recv_sem=sems.at[(1,) + where],
            device_id=device,
            device_id_type=MESH,
        )
        copy.start()
        started.append(copy)
        return copy

    if square_plane:
        flat, upright, across = q + 1 - 2 * (q % 2), q + 2 - 4 * (q // 2), 3 - q
        ahead = (q, flat, upright, across)
        behind = ahead
    else:
        ahead = tuple(lax.rem(q + k, chips) for k in range(chips))
        behind = tuple(lax.rem(q + chips - k, chips) for k in range(chips))

    def device_at(k):
        return (2 * ahead[k] + core, f)

    def mine_of(h, chip, cols):
        return kept[chip, h, :, cols].astype(f32) + pair[h, chip, :, cols].astype(f32)

    def rows_of(h, device):
        return pl.ds(pl.multiple_of((h * dp_count + device) * STEP, STEP), STEP)

    paired = [
        send(grad_all.at[:, 1 - core, h], pair.at[h], pair_sem, (h,), partner)
        for h in range(steps)
    ]
    everything = pl.ds(0, width)
    first = {}
    second = {}
    gathered = {}
    relayed = {}
    cored = {}
    grams_wide = {}
    grams = {}
    own_gram = {}
    square_sum = []

    def first_send(h):
        paired[h].wait_recv()
        if square_plane:
            for side, (k, cols) in enumerate(((1, left), (2, right))):
                for j, chip in enumerate((ahead[k], ahead[3])):
                    out_first[h, side, j] = mine_of(h, chip, cols).astype(bf16)
                first[h, side] = send(
                    out_first.at[h, side],
                    in_first.at[h, side],
                    first_sem,
                    (h, side),
                    device_at(k),
                )
        else:
            for k in range(1, chips):
                out_first[h, k] = mine_of(h, ahead[k], everything).astype(bf16)
                first[h, k] = send(
                    out_first.at[h, k], in_first.at[h, k], first_sem, (h, k), device_at(k)
                )

    def second_send(h):
        if square_plane:
            for side, (k, cols) in enumerate(((2, left), (1, right))):
                first[h, side].wait_recv()
                out_second[h, side] = (
                    mine_of(h, ahead[k], cols) + in_first[h, side, 1].astype(f32)
                ).astype(bf16)
                second[h, side] = send(
                    out_second.at[h, side],
                    in_second.at[h, side],
                    second_sem,
                    (h, side),
                    device_at(k),
                )

    def blend(h):
        if square_plane:
            parts = []
            for side, cols in enumerate((left, right)):
                second[h, side].wait_recv()
                parts.append(
                    (
                        cols,
                        mine_of(h, q, cols)
                        + in_first[h, side, 0].astype(f32)
                        + in_second[h, side].astype(f32),
                    )
                )
        else:
            summed = mine_of(h, q, everything)
            for k in range(1, chips):
                first[h, k].wait_recv()
                summed = summed + in_first[h, k].astype(f32)
            parts = [(everything, summed)]
        here = pl.ds(h * STEP, STEP)
        for cols, summed in parts:
            updated = momentum_decay * momentum[here, cols] + summed
            new_momentum[here, cols] = updated
            blended = summed + momentum_decay * updated
            columns[rows_of(h, d), cols] = blended.astype(bf16)
            square_sum.append(jnp.sum(blended * blended))
        mine = columns.at[rows_of(h, d)]
        for k in range(1, 3 if square_plane else chips):
            gathered[h, k] = send(mine, mine, gather_sem, (h, k), device_at(k))
        cored[h, 0] = send(mine, mine, core_sem, (h, 0), partner)

    def pass_on(h):
        for k in range(1, 3 if square_plane else chips):
            gathered[h, k].wait_recv()
            there = columns.at[rows_of(h, 2 * behind[k] + core)]
            if square_plane:
                part = columns.at[
                    rows_of(h, 2 * behind[k] + core), (left, right)[k - 1]
                ]
                relayed[h, k] = send(part, part, relay_sem, (h, k), device_at(3 - k))
            cored[h, k] = send(there, there, core_sem, (h, k), partner)

    def pass_diagonal(h):
        if square_plane:
            for k in (1, 2):
                relayed[h, k].wait_recv()
            there = columns.at[rows_of(h, 2 * across + core)]
            cored[h, 3] = send(there, there, core_sem, (h, 3), partner)

    def part_gram(h):
        for k in range(chips):
            cored[h, k].wait_recv()
        reach = (h + 1) * dp_count * STEP
        own_gram[h] = lax.dot_general(
            columns[rows_of(h, d)],
            columns[0:reach],
            (((1,), (1,)), ((), ())),
            preferred_element_type=f32,
        )
        gram_own[h, :, 0:reach] = own_gram[h].astype(bf16)
        for k in range(1, fsdp_count):
            grams_wide[h, k] = send(
                gram_own.at[h, :, pl.ds(0, reach)],
                gram_in.at[h, k, :, pl.ds(0, reach)],
                gram_wide_sem,
                (h, k),
                (d, lax.rem(f + k, fsdp_count)),
            )

    def whole_gram(h):
        reach = (h + 1) * dp_count * STEP
        total = own_gram[h]
        for k in range(1, fsdp_count):
            grams_wide[h, k].wait_recv()
            total = total + gram_in[h, k, :, 0:reach].astype(f32)
        gram[rows_of(h, d), 0:reach] = total.astype(bf16)
        mine = gram.at[rows_of(h, d), pl.ds(0, reach)]
        for k in range(1, dp_count):
            grams[h, k] = send(
                mine, mine, gram_sem, (h, k), (lax.rem(d + k, dp_count), f)
            )

    stat_copies = {}
    stat_wide_copies = {}

    def stats_send():
        total = square_sum[0]
        for value in square_sum[1:]:
            total = total + value
        peaks_copy.wait()
        stats_in[d] = jnp.full((8, 128), total, f32)
        stats_in[d, 0:1, 0:HEADS] = peaks[...].astype(f32)
        for k in range(1, dp_count):
            stat_copies[k] = send(
                stats_in.at[d],
                stats_in.at[d],
                stats_sem,
                (k,),
                (lax.rem(d + k, dp_count), f),
            )

    def stats_pass():
        for k in range(1, dp_count):
            stat_copies[k].wait_recv()
        stats_wide[f, 0:1] = functools.reduce(
            jnp.maximum, [stats_in[j, 0:1] for j in range(dp_count)]
        )
        stats_wide[f, 1:8] = sum(stats_in[j, 1:8] for j in range(dp_count))
        for k in range(1, fsdp_count):
            stat_wide_copies[k] = send(
                stats_wide.at[f],
                stats_wide.at[f],
                stats_wide_sem,
                (k,),
                (d, lax.rem(f + k, fsdp_count)),
            )

    def stats_end():
        for k in range(1, fsdp_count):
            stat_wide_copies[k].wait_recv()
        stats_out[0:1] = functools.reduce(
            jnp.maximum, [stats_wide[j, 0:1] for j in range(fsdp_count)]
        )
        stats_out[1:8] = sum(stats_wide[j, 1:8] for j in range(fsdp_count))

    kept_copy.wait()
    for h in range(steps):
        first_send(h)
    momentum_copy.wait()
    stages = (second_send, blend, pass_on, pass_diagonal, part_gram, whole_gram)
    for tick in range(steps + len(stages) - 1):
        for lag, stage in enumerate(stages):
            h = tick - lag
            if 0 <= h < steps:
                stage(h)
                if stage is blend and h == steps - 1:
                    stats_send()
                if stage is pass_on and h == steps - 1:
                    stats_pass()
    stats_end()
    for copy in grams.values():
        copy.wait_recv()
    for copy in started:
        copy.wait_send()


def reduce_and_gather(gradient, momentum, peaks):
    dp_count = lax.axis_size("dp")
    fsdp_count = lax.axis_size("fsdp")
    chips = dp_count // 2
    rows, width = momentum.shape
    steps = rows // STEP
    half = width // 2
    square_plane = chips == 4
    gradient = gradient.reshape(chips, 2, steps, STEP, width)
    in_hbm = pl.BlockSpec(memory_space=pltpu.HBM)
    in_vmem = pl.BlockSpec(memory_space=pltpu.VMEM)
    if square_plane:
        first = (steps, 2, 2, STEP, half)
        second = (steps, 2, STEP, half)
    else:
        first = (steps, chips, STEP, width)
        second = (1, 1, STEP, 128)
    dma = pltpu.SemaphoreType.DMA
    return pl.pallas_call(
        functools.partial(exchange, dp_count, fsdp_count),
        out_shape=(
            jax.ShapeDtypeStruct((rows, width), f32),
            jax.ShapeDtypeStruct((KVL, width), bf16),
            jax.ShapeDtypeStruct((KVL, KVL), bf16),
            jax.ShapeDtypeStruct((8, 128), f32),
        ),
        in_specs=[in_hbm] * 3,
        out_specs=(in_vmem,) * 4,
        scratch_shapes=[
            pltpu.VMEM((chips, steps, STEP, width), bf16),
            pltpu.VMEM((steps, chips, STEP, width), bf16),
            pltpu.VMEM((rows, width), f32),
            pltpu.VMEM((1, HEADS), jnp.int32),
            pltpu.VMEM(first, bf16),
            pltpu.VMEM(first, bf16),
            pltpu.VMEM(second, bf16),
            pltpu.VMEM(second, bf16),
            pltpu.VMEM((steps, STEP, KVL), bf16),
            pltpu.VMEM((steps, fsdp_count, STEP, KVL), bf16),
            pltpu.VMEM((dp_count, 8, 128), f32),
            pltpu.VMEM((fsdp_count, 8, 128), f32),
            dma((3,)),
            dma((2, steps)),
            dma((2, steps, max(chips, 2))),
            dma((2, steps, 2)),
            dma((2, steps, chips)),
            dma((2, steps, 3)),
            dma((2, steps, chips)),
            dma((2, steps, fsdp_count)),
            dma((2, steps, dp_count)),
            dma((2, dp_count)),
            dma((2, fsdp_count)),
        ],
        compiler_params=pltpu.CompilerParams(
            collective_id=0, has_side_effects=True, vmem_limit_bytes=40 * 1024 * 1024
        ),
    )(gradient, momentum, peaks)


def product(left, right):
    return jnp.dot(left.astype(bf16), right.astype(bf16), preferred_element_type=f32)


def careful_product(left, right):
    high = right.astype(bf16)
    low = (right - high.astype(f32)).astype(bf16)
    left = left.astype(bf16)
    return jnp.dot(left, high, preferred_element_type=f32) + jnp.dot(
        left, low, preferred_element_type=f32
    )


def finish(
    dp_count,
    new_momentum,
    columns,
    gram,
    stats,
    weight_all,
    clip_all,
    new_weight_all,
    new_momentum_all,
    update_norm,
    weight,
    new_weight,
    clip,
    full_gram,
    small_sem,
    weight_sem,
    out_sem,
):
    rows, width = new_momentum.shape
    steps = rows // STEP
    span = NOPE + VDIM
    heads = width // span
    lead, second, third = quintic_terms
    clip_copy = pltpu.make_async_copy(clip_all, clip, small_sem.at[0])
    clip_copy.start()
    weight_copies = []
    for j in range(heads):
        cols = pl.ds(j * span, span)
        copy = pltpu.make_async_copy(weight_all.at[:, cols], weight.at[:, cols], weight_sem.at[j])
        copy.start()
        weight_copies.append(copy)
    momentum_copy = pltpu.make_async_copy(new_momentum, new_momentum_all, small_sem.at[1])
    momentum_copy.start()

    block = dp_count * STEP
    for i in range(steps):
        reach = (i + 1) * block
        full_gram[i * block : reach, 0:reach] = gram[i * block : reach, 0:reach]
        for j in range(i):
            piece = gram[i * block : reach, j * block : (j + 1) * block].astype(f32)
            full_gram[j * block : (j + 1) * block, i * block : reach] = piece.T.astype(bf16)

    level = stats[1:2, 0:1]
    update_norm[0] = jnp.sqrt(level * (1.0 / (KVL * KVO)))[0, 0]
    inverse = 1.0 / (jnp.sqrt(level) + epsilon)
    scale = inverse * inverse
    whole = None
    total = full_gram[...]
    gram_now = total.astype(f32) * scale
    square = (scale * scale) * jnp.dot(total, total, preferred_element_type=f32)
    for iteration in range(ITERS):
        last = iteration == ITERS - 1
        rest = second * gram_now + third * (
            square if iteration == 0 else product(gram_now, gram_now)
        )
        if whole is None:
            row = lax.broadcasted_iota(jnp.int32, (KVL, KVL), 0)
            col = lax.broadcasted_iota(jnp.int32, (KVL, KVL), 1)
            whole = jnp.where(row == col, lead, 0.0) + rest
        else:
            whole = lead * whole + (careful_product if last else product)(rest, whole)
        if not last:
            part = lead * gram_now + product(rest, gram_now)
            gram_now = lead * part + product(part, rest)
    whole = whole.astype(bf16)

    clip_copy.wait()
    threshold = clip[0].astype(f32)
    factors = jnp.sqrt(jnp.minimum(1.0, threshold / stats[0:1]))
    lane = lax.broadcasted_iota(jnp.int32, (1, 128), 1)
    first_head = lax.axis_index("fsdp") * heads
    update_scale = (learning_rate * update_gain * math.sqrt(max(KVL, KVO))) * inverse
    out_copies = []
    for j in range(heads):
        weight_copies[j].wait()
        cols = pl.ds(j * span, span)
        factor = jnp.sum(jnp.where(lane == first_head + j, factors, 0.0), axis=1, keepdims=True)
        orthogonal = jnp.dot(whole, columns[:, cols], preferred_element_type=f32)
        key_cols = lax.broadcasted_iota(jnp.int32, (1, span), 1) < NOPE
        keep = jnp.where(key_cols, factor * (1.0 - learning_rate * weight_decay), 1.0 - learning_rate * weight_decay)
        move = jnp.where(key_cols, factor * update_scale, update_scale)
        for h in range(steps):
            for device in range(dp_count):
                here = pl.ds(device * rows + h * STEP, STEP)
                start = (h * dp_count + device) * STEP
                new_weight[here, cols] = (
                    keep * weight[here, cols] - move * orthogonal[start : start + STEP]
                )
        copy = pltpu.make_async_copy(
            new_weight.at[:, cols], new_weight_all.at[:, cols], out_sem.at[j]
        )
        copy.start()
        out_copies.append(copy)
    momentum_copy.wait()
    for copy in out_copies:
        copy.wait()


def polish(new_momentum, columns, gram, stats, weight, clip_threshold):
    dp_count = lax.axis_size("dp")
    rows, width = new_momentum.shape
    heads = width // (NOPE + VDIM)
    in_hbm = pl.BlockSpec(memory_space=pltpu.HBM)
    in_vmem = pl.BlockSpec(memory_space=pltpu.VMEM)
    dma = pltpu.SemaphoreType.DMA
    return pl.pallas_call(
        functools.partial(finish, dp_count),
        out_shape=(
            jax.ShapeDtypeStruct((KVL, width), f32),
            jax.ShapeDtypeStruct((rows, width), f32),
            jax.ShapeDtypeStruct((1,), f32),
        ),
        in_specs=[in_vmem] * 4 + [in_hbm] * 2,
        out_specs=(in_hbm, in_hbm, pl.BlockSpec(memory_space=pltpu.SMEM)),
        scratch_shapes=[
            pltpu.VMEM((KVL, width), f32),
            pltpu.VMEM((KVL, width), f32),
            pltpu.SMEM((1,), jnp.int32),
            pltpu.VMEM((KVL, KVL), bf16),
            dma((2,)),
            dma((heads,)),
            dma((heads,)),
        ],
        compiler_params=pltpu.CompilerParams(vmem_limit_bytes=40 * 1024 * 1024),
    )(new_momentum, columns, gram, stats, weight, clip_threshold)


def local(gradients, momentum, weight, logit_peaks, clip_threshold):
    exchanged = reduce_and_gather(gradients, momentum, logit_peaks)
    return polish(*exchanged, weight, clip_threshold)


def solution(mesh):
    placed = (P("dp", None, "fsdp"), P("dp", "fsdp"), P(None, "fsdp"), P(("dp", "fsdp"), None), P())
    return jax.shard_map(
        local,
        mesh=mesh,
        in_specs=placed,
        out_specs=(P(None, "fsdp"), P("dp", "fsdp"), P()),
        check_vma=False,
    )
```

```python
import functools
import math

import jax
import jax.numpy as jnp
from jax import lax
from jax.experimental import pallas as pl
from jax.experimental.pallas import tpu as pltpu
from jax.sharding import PartitionSpec as P

KVL = 512
NOPE = 128
VDIM = 128
HEADS = 32
ITERS = 3
KVO = 8192


quintic_terms = (3.4445, -4.775, 2.0315)
learning_rate = 0.5
weight_decay = 0.1
momentum_decay = 0.95
update_gain = 0.2
epsilon = 1e-07

STEP = 16
SENDERS = 11
GROUP = 1
ORDER = "F0 F1 F2 F3 S0 S1 S2 S3 B0 B1 B2 B3 T P0 P1 P2 P3 D0 D1 G0 D2 G1 G2 G3 D3 C U Z0 Z1 Z2 Z3 E"
MESH = pl.DeviceIdType.MESH
f32 = jnp.float32
bf16 = jnp.bfloat16


def pieces_of(steps):
    last = steps - 1
    whole = [(h, 0, h + 1) for h in range(last)]
    return whole + [(last, 0, last if last else 1)]


def order_of(steps):
    assert steps in (1, 4)
    if steps == 4:
        return ORDER.split()
    last = len(pieces_of(steps))
    stages = [[kind + str(h) for h in range(steps)] for kind in "FSBPD"]
    grams = [[kind + str(piece) for piece in range(last)] for kind in "GZ"]
    return sum(stages[:3], []) + ["T"] + sum(stages[3:], []) + ["U"] + sum(grams, [])


def exchange(
    dp_count,
    fsdp_count,
    grad_all,
    momentum_all,
    peaks_all,
    new_momentum,
    columns,
    gram,
    stats_out,
    kept,
    pair,
    momentum,
    peaks,
    out_first,
    in_first,
    out_second,
    in_second,
    gram_own,
    gram_in,
    stats_in,
    stats_wide,
    local_sem,
    sent_sem,
    pair_sem,
    first_sem,
    second_sem,
    gather_sem,
    relay_sem,
    core_sem,
    gram_wide_sem,
    last_sem,
    corner_own,
    corner_in,
):
    d = lax.axis_index("dp")
    f = lax.axis_index("fsdp")
    chips = dp_count // 2
    q = d // 2
    core = d % 2
    steps = kept.shape[0]
    width = momentum.shape[1]
    half = width // 2
    left = pl.ds(0, half)
    right = pl.ds(half, half)
    square_plane = chips == 4
    partner = (2 * q + 1 - core, f)

    barrier = pltpu.get_barrier_semaphore()
    for k in range(1, dp_count):
        pl.semaphore_signal(
            barrier, inc=1, device_id=(lax.rem(d + k, dp_count), f), device_id_type=MESH
        )
    for k in range(1, fsdp_count):
        pl.semaphore_signal(
            barrier, inc=1, device_id=(d, lax.rem(f + k, fsdp_count)), device_id_type=MESH
        )
    kept_copies = [
        pltpu.make_async_copy(grad_all.at[:, core, h], kept.at[h], local_sem.at[h])
        for h in range(steps)
    ]
    momentum_copy = pltpu.make_async_copy(momentum_all, momentum, local_sem.at[steps])
    peaks_copy = pltpu.make_async_copy(peaks_all, peaks, local_sem.at[steps + 1])
    for copy in kept_copies + [momentum_copy, peaks_copy]:
        copy.start()
    pl.semaphore_wait(barrier, dp_count + fsdp_count - 2)

    volume = [0] * SENDERS

    def send(source, target, sender, arrival, device):
        volume[sender] += math.prod(source.shape)
        pltpu.make_async_remote_copy(
            src_ref=source,
            dst_ref=target,
            send_sem=sent_sem.at[sender],
            recv_sem=arrival,
            device_id=device,
            device_id_type=MESH,
        ).start()

    def wait_for(like, arrival):
        pltpu.make_async_copy(like, like, arrival).wait()

    def stripes(count):
        lanes = count // STEP
        cols = max(c for c in range(128, width + 1, 128) if lanes % c == 0)
        return columns.at[pl.ds(0, lanes // cols * STEP), pl.ds(0, cols)]

    if square_plane:
        flat, upright, across = q + 1 - 2 * (q % 2), q + 2 - 4 * (q // 2), 3 - q
        ahead = (q, flat, upright, across)
        behind = ahead
    else:
        ahead = tuple(lax.rem(q + k, chips) for k in range(chips))
        behind = tuple(lax.rem(q + chips - k, chips) for k in range(chips))

    def device_at(k):
        return (2 * ahead[k] + core, f)

    def mine_of(h, chip, cols):
        return kept[h, chip, :, cols].astype(f32) + pair[h, chip, :, cols].astype(f32)

    def rows_of(h, device):
        return pl.ds(pl.multiple_of((h * dp_count + device) * STEP, STEP), STEP)

    for h in range(steps):
        send(grad_all.at[:, 1 - core, h], pair.at[h], 0, pair_sem.at[h], partner)
    everything = pl.ds(0, width)
    own_gram = {}
    block = dp_count * STEP
    pieces = pieces_of(steps)
    square_sum = []

    def first_send(h):
        kept_copies[h].wait()
        wait_for(pair.at[h], pair_sem.at[h])
        if square_plane:
            for side, (k, cols) in enumerate(((1, left), (2, right))):
                for j, chip in enumerate((ahead[k], ahead[3])):
                    out_first[h, side, j] = mine_of(h, chip, cols).astype(bf16)
                send(
                    out_first.at[h, side],
                    in_first.at[h, side],
                    1,
                    first_sem.at[h],
                    device_at(k),
                )
        else:
            for k in range(1, chips):
                out_first[h, k - 1] = mine_of(h, ahead[k], everything).astype(bf16)
                send(
                    out_first.at[h, k - 1],
                    in_first.at[h, k - 1],
                    1,
                    first_sem.at[h],
                    device_at(k),
                )

    def second_send(h):
        wait_for(in_first.at[h], first_sem.at[h])
        if square_plane:
            for side, (k, cols) in enumerate(((2, left), (1, right))):
                out_second[h, side] = (
                    mine_of(h, ahead[k], cols) + in_first[h, side, 1].astype(f32)
                ).astype(bf16)
                send(
                    out_second.at[h, side],
                    in_second.at[h, side],
                    2,
                    second_sem.at[h],
                    device_at(k),
                )

    def blend(h):
        if square_plane:
            parts = []
            wait_for(in_second.at[h], second_sem.at[h])
            for side, cols in enumerate((left, right)):
                parts.append(
                    (
                        cols,
                        mine_of(h, q, cols)
                        + in_first[h, side, 0].astype(f32)
                        + in_second[h, side].astype(f32),
                    )
                )
        else:
            summed = mine_of(h, q, everything)
            for k in range(1, chips):
                summed = summed + in_first[h, k - 1].astype(f32)
            parts = [(everything, summed)]
        if h == 0:
            momentum_copy.wait()
        here = pl.ds(h * STEP, STEP)
        for cols, summed in parts:
            updated = momentum_decay * momentum[here, cols] + summed
            new_momentum[here, cols] = updated
            blended = summed + momentum_decay * updated
            columns[rows_of(h, d), cols] = blended.astype(bf16)
            square_sum.append(jnp.sum(blended * blended))
        mine = columns.at[rows_of(h, d)]
        for k in range(1, 3 if square_plane else chips):
            send(mine, mine, 3, gather_sem.at[h], device_at(k))
        send(mine, mine, 5, core_sem.at[h], partner)

    def pass_on(h):
        near = range(1, 3 if square_plane else chips)
        wait_for(stripes(len(near) * STEP * width), gather_sem.at[h])
        for k in near:
            there = columns.at[rows_of(h, 2 * behind[k] + core)]
            if square_plane:
                part = columns.at[
                    rows_of(h, 2 * behind[k] + core), (left, right)[k - 1]
                ]
                send(part, part, 4, relay_sem.at[h], device_at(3 - k))
            send(there, there, 5, core_sem.at[h], partner)

    def pass_diagonal(h):
        if square_plane:
            there = columns.at[rows_of(h, 2 * across + core)]
            wait_for(there, relay_sem.at[h])
            send(there, there, 5, core_sem.at[h], partner)

    def part_gram(piece):
        h, low, high = pieces[piece]
        if high == h + 1:
            wait_for(stripes(chips * STEP * width), core_sem.at[h])
        own_gram[piece] = lax.dot_general(
            columns[rows_of(h, d)],
            columns[low * block : high * block],
            (((1,), (1,)), ((), ())),
            preferred_element_type=f32,
        )
        reach = pl.ds(low * block, (high - low) * block)
        gram_own[h, :, reach] = own_gram[piece].astype(bf16)
        for k in range(1, fsdp_count):
            send(
                gram_own.at[h, :, reach],
                gram_in.at[h, k - 1, :, reach],
                6,
                gram_wide_sem.at[piece],
                (d, lax.rem(f + k, fsdp_count)),
            )

    def whole_gram(piece):
        h, low, high = pieces[piece]
        reach = pl.ds(low * block, (high - low) * block)
        total = own_gram[piece]
        wait_for(gram_in.at[h, :, :, reach], gram_wide_sem.at[piece])
        for k in range(1, fsdp_count):
            total = total + gram_in[h, k - 1, :, reach].astype(f32)
        gram[rows_of(h, d), reach] = total.astype(bf16)
        mine = gram.at[rows_of(h, d), reach]
        for k in range(1, dp_count):
            send(mine, mine, 7, last_sem.at[0], (lax.rem(d + k, dp_count), f))

    corner = pl.ds((steps - 1) * block, block)
    corner_total = {}
    middle = block // 2
    quarter = block // 4

    def part_corner():
        wait_for(stripes(chips * STEP * width), core_sem.at[steps - 1])
        newest = columns[corner]
        full = lax.dot_general(
            newest, newest, (((1,), (1,)), ((), ())), preferred_element_type=f32
        )
        packed = jnp.concatenate(
            [
                full[middle:block],
                jnp.concatenate([full[0:quarter, 0:middle], full[quarter:middle, 0:middle]], axis=1),
            ],
            axis=0,
        )
        corner_total[0] = packed
        corner_own[...] = packed.astype(bf16)
        for k in range(1, fsdp_count):
            send(
                corner_own,
                corner_in.at[k - 1],
                10,
                last_sem.at[3],
                (d, lax.rem(f + k, fsdp_count)),
            )

    def whole_corner():
        wait_for(corner_in, last_sem.at[3])
        total = corner_total[0]
        for k in range(1, fsdp_count):
            total = total + corner_in[k - 1].astype(f32)
        total = total.astype(bf16).astype(f32)
        first_half = jnp.concatenate(
            [total[middle:, 0:middle], total[middle:, middle:block]], axis=0
        )
        first_half = jnp.concatenate([first_half, jnp.zeros_like(first_half)], axis=1)
        gram[pl.ds(corner.start, middle), corner] = first_half.astype(bf16)
        gram[pl.ds(corner.start + middle, middle), corner] = total[0:middle].astype(bf16)

    def stats_send():
        total = square_sum[0]
        for value in square_sum[1:]:
            total = total + value
        peaks_copy.wait()
        stats_in[d] = jnp.full((8, 128), total, f32)
        stats_in[d, 0:1, 0:HEADS] = peaks[...].astype(f32)
        for k in range(1, dp_count):
            send(
                stats_in.at[d],
                stats_in.at[d],
                8,
                last_sem.at[1],
                (lax.rem(d + k, dp_count), f),
            )

    def stats_pass():
        wait_for(stats_in.at[pl.ds(0, dp_count - 1)], last_sem.at[1])
        stats_wide[f, 0:1] = functools.reduce(
            jnp.maximum, [stats_in[j, 0:1] for j in range(dp_count)]
        )
        stats_wide[f, 1:8] = sum(stats_in[j, 1:8] for j in range(dp_count))
        for k in range(1, fsdp_count):
            send(
                stats_wide.at[f],
                stats_wide.at[f],
                9,
                last_sem.at[2],
                (d, lax.rem(f + k, fsdp_count)),
            )

    def stats_end():
        wait_for(stats_wide.at[pl.ds(0, fsdp_count - 1)], last_sem.at[2])
        stats_out[0:1] = functools.reduce(
            jnp.maximum, [stats_wide[j, 0:1] for j in range(fsdp_count)]
        )
        stats_out[1:8] = sum(stats_wide[j, 1:8] for j in range(fsdp_count))

    acts = {
        "F": first_send,
        "S": second_send,
        "B": blend,
        "P": pass_on,
        "D": pass_diagonal,
        "G": part_gram,
        "Z": whole_gram,
        "C": part_corner,
        "E": whole_corner,
        "T": stats_send,
        "U": stats_pass,
    }
    for act in order_of(steps):
        acts[act[0]](*(int(digit) for digit in act[1:]))
    stats_end()
    wait_for(stripes(volume[7]), last_sem.at[0])
    if volume[10]:
        wait_for(corner_in, sent_sem.at[10])
    for sender in range(8):
        if volume[sender]:
            wait_for(stripes(volume[sender]), sent_sem.at[sender])
    wait_for(stats_in.at[pl.ds(0, dp_count - 1)], sent_sem.at[8])
    wait_for(stats_wide.at[pl.ds(0, fsdp_count - 1)], sent_sem.at[9])


def reduce_and_gather(gradient, momentum, peaks):
    dp_count = lax.axis_size("dp")
    fsdp_count = lax.axis_size("fsdp")
    chips = dp_count // 2
    rows, width = momentum.shape
    steps = rows // STEP
    half = width // 2
    square_plane = chips == 4
    gradient = gradient.reshape(chips, 2, steps, STEP, width)
    in_hbm = pl.BlockSpec(memory_space=pltpu.HBM)
    in_vmem = pl.BlockSpec(memory_space=pltpu.VMEM)
    if square_plane:
        first = (steps, 2, 2, STEP, half)
        second = (steps, 2, STEP, half)
    else:
        first = (steps, chips - 1, STEP, width)
        second = (1, 1, STEP, 128)
    dma = pltpu.SemaphoreType.DMA
    return pl.pallas_call(
        functools.partial(exchange, dp_count, fsdp_count),
        out_shape=(
            pltpu.VMEM((rows, width), f32),
            pltpu.VMEM((KVL, width), bf16),
            pltpu.VMEM((KVL, KVL), bf16),
            pltpu.VMEM((8, 128), f32),
        ),
        in_specs=[in_hbm] * 3,
        out_specs=(in_vmem,) * 4,
        scratch_shapes=[
            pltpu.VMEM((steps, chips, STEP, width), bf16),
            pltpu.VMEM((steps, chips, STEP, width), bf16),
            pltpu.VMEM((rows, width), f32),
            pltpu.VMEM((1, HEADS), jnp.int32),
            pltpu.VMEM(first, bf16),
            pltpu.VMEM(first, bf16),
            pltpu.VMEM(second, bf16),
            pltpu.VMEM(second, bf16),
            pltpu.VMEM((steps, STEP, KVL), bf16),
            pltpu.VMEM((steps, fsdp_count - 1, STEP, KVL), bf16),
            pltpu.VMEM((dp_count, 8, 128), f32),
            pltpu.VMEM((fsdp_count, 8, 128), f32),
            dma((steps + 2,)),
            dma((SENDERS,)),
            dma((steps,)),
            dma((steps,)),
            dma((steps,)),
            dma((steps,)),
            dma((steps,)),
            dma((steps,)),
            dma((len(pieces_of(steps)),)),
            dma((4,)),
            pltpu.VMEM((dp_count * STEP * 3 // 4, dp_count * STEP), bf16),
            pltpu.VMEM((fsdp_count - 1, dp_count * STEP * 3 // 4, dp_count * STEP), bf16),
        ],
        compiler_params=pltpu.CompilerParams(
            collective_id=0, has_side_effects=True, vmem_limit_bytes=24 * 1024 * 1024
        ),
        cost_estimate=pl.CostEstimate(
            flops=40_000_000_000, bytes_accessed=4_000_000, transcendentals=0
        ),
    )(*(pltpu.with_memory_space_constraint(x, pltpu.HBM) for x in (gradient, momentum, peaks)))


def product(left, right):
    return jnp.dot(left.astype(bf16), right.astype(bf16), preferred_element_type=f32)


def careful_product(left, right):
    high = right.astype(bf16)
    low = (right - high.astype(f32)).astype(bf16)
    left = left.astype(bf16)
    return jnp.dot(left, high, preferred_element_type=f32) + jnp.dot(
        left, low, preferred_element_type=f32
    )


def finish(
    dp_count,
    new_momentum,
    columns,
    gram,
    stats,
    weight,
    clip_all,
    new_weight_all,
    new_momentum_all,
    update_norm,
    new_weight,
    clip,
    full_gram,
    small_sem,
    out_sem,
):
    rows, width = new_momentum.shape
    steps = rows // STEP
    span = NOPE + VDIM
    heads = width // span
    lead, second, third = quintic_terms
    clip_copy = pltpu.make_async_copy(clip_all, clip, small_sem.at[0])
    clip_copy.start()
    momentum_copy = pltpu.make_async_copy(new_momentum, new_momentum_all, small_sem.at[1])
    momentum_copy.start()

    block = dp_count * STEP
    for i in range(steps):
        reach = (i + 1) * block
        full_gram[i * block : reach, 0:reach] = gram[i * block : reach, 0:reach]
        if i and i == steps - 1:
            middle = reach - block // 2
            piece = gram[middle:reach, i * block : middle].astype(f32)
            full_gram[i * block : middle, middle:reach] = piece.T.astype(bf16)
        for j in range(i):
            piece = gram[i * block : reach, j * block : (j + 1) * block].astype(f32)
            full_gram[j * block : (j + 1) * block, i * block : reach] = piece.T.astype(bf16)

    level = stats[1:2, 0:1]
    update_norm[0] = jnp.sqrt(level * (1.0 / (KVL * KVO)))[0, 0]
    inverse = 1.0 / (jnp.sqrt(level) + epsilon)
    scale = inverse * inverse
    whole = None
    total = full_gram[...]
    gram_now = total.astype(f32) * scale
    square = (scale * scale) * jnp.dot(total, total, preferred_element_type=f32)
    for iteration in range(ITERS):
        last = iteration == ITERS - 1
        rest = second * gram_now + third * (
            square if iteration == 0 else product(gram_now, gram_now)
        )
        if whole is None:
            row = lax.broadcasted_iota(jnp.int32, (KVL, KVL), 0)
            col = lax.broadcasted_iota(jnp.int32, (KVL, KVL), 1)
            whole = jnp.where(row == col, lead, 0.0) + rest
        else:
            whole = lead * whole + (careful_product if last else product)(rest, whole)
        if not last:
            part = lead * gram_now + product(rest, gram_now)
            gram_now = lead * part + product(part, rest)
    whole = whole.astype(bf16)

    clip_copy.wait()
    threshold = clip[0].astype(f32)
    factors = jnp.sqrt(jnp.minimum(1.0, threshold / stats[0:1]))
    lane = lax.broadcasted_iota(jnp.int32, (1, 128), 1)
    first_head = lax.axis_index("fsdp") * heads
    update_scale = (learning_rate * update_gain * math.sqrt(max(KVL, KVO))) * inverse
    factor_row = jnp.concatenate(
        [
            piece
            for j in range(heads)
            for piece in (
                jnp.broadcast_to(
                    jnp.sum(
                        jnp.where(lane == first_head + j, factors, 0.0), axis=1, keepdims=True
                    ),
                    (1, NOPE),
                ),
                jnp.ones((1, VDIM), f32),
            )
        ],
        axis=1,
    )
    keep = factor_row * (1.0 - learning_rate * weight_decay)
    move = factor_row * update_scale
    out_copies = []
    group = min(GROUP, steps)
    for g in range(steps // group):
        rows_now = whole[g * group * block : (g + 1) * group * block]
        for j in range(width // span):
            cols = pl.ds(j * span, span)
            orthogonal = jnp.dot(rows_now, columns[:, cols], preferred_element_type=f32)
            for i in range(group):
                h = g * group + i
                for device in range(dp_count):
                    start = (i * dp_count + device) * STEP
                    new_weight[device, h, :, cols] = (
                        keep[:, j * span : (j + 1) * span] * weight[device, h, :, cols]
                        - move[:, j * span : (j + 1) * span] * orthogonal[start : start + STEP]
                    )
        here = pl.ds(g * group, group)
        copy = pltpu.make_async_copy(
            new_weight.at[:, here], new_weight_all.at[:, here], out_sem.at[g]
        )
        copy.start()
        out_copies.append(copy)
    momentum_copy.wait()
    for copy in out_copies:
        copy.wait()


def polish(new_momentum, columns, gram, stats, weight, clip_threshold):
    dp_count = lax.axis_size("dp")
    rows, width = new_momentum.shape
    steps = rows // STEP
    in_hbm = pl.BlockSpec(memory_space=pltpu.HBM)
    in_vmem = pl.BlockSpec(memory_space=pltpu.VMEM)
    dma = pltpu.SemaphoreType.DMA
    weight = weight.reshape(dp_count, steps, STEP, width)
    new_weight, new_momentum, update_norm = pl.pallas_call(
        functools.partial(finish, dp_count),
        out_shape=(
            jax.ShapeDtypeStruct((dp_count, steps, STEP, width), f32),
            jax.ShapeDtypeStruct((rows, width), f32),
            jax.ShapeDtypeStruct((1,), f32),
        ),
        in_specs=[in_vmem] * 5 + [in_hbm],
        out_specs=(in_hbm, in_hbm, pl.BlockSpec(memory_space=pltpu.SMEM)),
        scratch_shapes=[
            pltpu.VMEM((dp_count, steps, STEP, width), f32),
            pltpu.SMEM((1,), jnp.int32),
            pltpu.VMEM((KVL, KVL), bf16),
            dma((2,)),
            dma((steps,)),
        ],
        compiler_params=pltpu.CompilerParams(vmem_limit_bytes=24 * 1024 * 1024),
    )(new_momentum, columns, gram, stats, weight, clip_threshold)
    return new_weight.reshape(KVL, width), new_momentum, update_norm


def local(gradients, momentum, weight, logit_peaks, clip_threshold):
    exchanged = reduce_and_gather(gradients, momentum, logit_peaks)
    return polish(*exchanged, weight, clip_threshold)


def solution(mesh):
    placed = (P("dp", None, "fsdp"), P("dp", "fsdp"), P(None, "fsdp"), P(("dp", "fsdp"), None), P())
    return jax.shard_map(
        local,
        mesh=mesh,
        in_specs=placed,
        out_specs=(P(None, "fsdp"), P("dp", "fsdp"), P()),
        check_vma=False,
    )
```

```python
import functools
import math

import jax
import jax.numpy as jnp
from jax import lax
from jax.experimental import pallas as pl
from jax.experimental.pallas import tpu as pltpu
from jax.sharding import PartitionSpec as P

KVL = 512
NOPE = 128
VDIM = 128
HEADS = 32
ITERS = 3
KVO = 8192


quintic_terms = (3.4445, -4.775, 2.0315)
learning_rate = 0.5
weight_decay = 0.1
momentum_decay = 0.95
update_gain = 0.2
epsilon = 1e-07

STEP = 16
SENDERS = 11
GROUP = 1
ORDER = "F0 F1 F2 F3 S0 S1 S2 S3 B0 B1 B2 P0 B3 T P1 P2 D0 P3 D1 G0 D2 G1 G2 G3 D3 C U Z0 Z1 Z2 Z3 E"
MESH = pl.DeviceIdType.MESH
f32 = jnp.float32
bf16 = jnp.bfloat16


def pieces_of(steps):
    last = steps - 1
    whole = [(h, 0, h + 1) for h in range(last)]
    return whole + [(last, 0, last if last else 1)]


def order_of(steps):
    assert steps in (1, 4)
    if steps == 4:
        return ORDER.split()
    last = len(pieces_of(steps))
    stages = [[kind + str(h) for h in range(steps)] for kind in "FSBPD"]
    grams = [[kind + str(piece) for piece in range(last)] for kind in "GZ"]
    return sum(stages[:3], []) + ["T"] + sum(stages[3:], []) + ["U"] + sum(grams, [])


def exchange(
    dp_count,
    fsdp_count,
    grad_all,
    momentum_all,
    peaks_all,
    new_momentum,
    columns,
    gram,
    stats_out,
    kept,
    pair,
    momentum,
    peaks,
    out_first,
    in_first,
    out_second,
    in_second,
    gram_own,
    gram_in,
    stats_in,
    stats_wide,
    local_sem,
    sent_sem,
    pair_sem,
    first_sem,
    second_sem,
    gather_sem,
    relay_sem,
    core_sem,
    gram_wide_sem,
    last_sem,
    corner_own,
    corner_in,
):
    d = lax.axis_index("dp")
    f = lax.axis_index("fsdp")
    chips = dp_count // 2
    q = d // 2
    core = d % 2
    steps = kept.shape[0]
    width = momentum.shape[1]
    half = width // 2
    left = pl.ds(0, half)
    right = pl.ds(half, half)
    square_plane = chips == 4
    partner = (2 * q + 1 - core, f)

    barrier = pltpu.get_barrier_semaphore()
    for k in range(1, dp_count):
        pl.semaphore_signal(
            barrier, inc=1, device_id=(lax.rem(d + k, dp_count), f), device_id_type=MESH
        )
    for k in range(1, fsdp_count):
        pl.semaphore_signal(
            barrier, inc=1, device_id=(d, lax.rem(f + k, fsdp_count)), device_id_type=MESH
        )
    kept_copies = [
        pltpu.make_async_copy(grad_all.at[:, core, h], kept.at[h], local_sem.at[h])
        for h in range(steps)
    ]
    momentum_copy = pltpu.make_async_copy(momentum_all, momentum, local_sem.at[steps])
    peaks_copy = pltpu.make_async_copy(peaks_all, peaks, local_sem.at[steps + 1])
    for copy in kept_copies + [momentum_copy, peaks_copy]:
        copy.start()
    pl.semaphore_wait(barrier, dp_count + fsdp_count - 2)

    volume = [0] * SENDERS

    def send(source, target, sender, arrival, device):
        volume[sender] += math.prod(source.shape)
        pltpu.make_async_remote_copy(
            src_ref=source,
            dst_ref=target,
            send_sem=sent_sem.at[sender],
            recv_sem=arrival,
            device_id=device,
            device_id_type=MESH,
        ).start()

    def wait_for(like, arrival):
        pltpu.make_async_copy(like, like, arrival).wait()

    def stripes(count):
        lanes = count // STEP
        cols = max(c for c in range(128, width + 1, 128) if lanes % c == 0)
        return columns.at[pl.ds(0, lanes // cols * STEP), pl.ds(0, cols)]

    if square_plane:
        flat, upright, across = q + 1 - 2 * (q % 2), q + 2 - 4 * (q // 2), 3 - q
        ahead = (q, flat, upright, across)
        behind = ahead
    else:
        ahead = tuple(lax.rem(q + k, chips) for k in range(chips))
        behind = tuple(lax.rem(q + chips - k, chips) for k in range(chips))

    def device_at(k):
        return (2 * ahead[k] + core, f)

    def mine_of(h, chip, cols):
        return kept[h, chip, :, cols].astype(f32) + pair[h, chip, :, cols].astype(f32)

    def rows_of(h, device):
        return pl.ds(pl.multiple_of((h * dp_count + device) * STEP, STEP), STEP)

    for h in range(steps):
        send(grad_all.at[:, 1 - core, h], pair.at[h], 0, pair_sem.at[h], partner)
    everything = pl.ds(0, width)
    own_gram = {}
    block = dp_count * STEP
    pieces = pieces_of(steps)
    square_sum = []

    def first_send(h):
        kept_copies[h].wait()
        wait_for(pair.at[h], pair_sem.at[h])
        if square_plane:
            for side, (k, cols) in enumerate(((1, left), (2, right))):
                for j, chip in enumerate((ahead[k], ahead[3])):
                    out_first[h, side, j] = mine_of(h, chip, cols).astype(bf16)
                send(
                    out_first.at[h, side],
                    in_first.at[h, side],
                    1,
                    first_sem.at[h],
                    device_at(k),
                )
        else:
            for k in range(1, chips):
                out_first[h, k - 1] = mine_of(h, ahead[k], everything).astype(bf16)
                send(
                    out_first.at[h, k - 1],
                    in_first.at[h, k - 1],
                    1,
                    first_sem.at[h],
                    device_at(k),
                )

    def second_send(h):
        wait_for(in_first.at[h], first_sem.at[h])
        if square_plane:
            for side, (k, cols) in enumerate(((2, left), (1, right))):
                out_second[h, side] = (
                    mine_of(h, ahead[k], cols) + in_first[h, side, 1].astype(f32)
                ).astype(bf16)
                send(
                    out_second.at[h, side],
                    in_second.at[h, side],
                    2,
                    second_sem.at[h],
                    device_at(k),
                )

    def blend(h):
        if square_plane:
            parts = []
            wait_for(in_second.at[h], second_sem.at[h])
            for side, cols in enumerate((left, right)):
                parts.append(
                    (
                        cols,
                        mine_of(h, q, cols)
                        + in_first[h, side, 0].astype(f32)
                        + in_second[h, side].astype(f32),
                    )
                )
        else:
            summed = mine_of(h, q, everything)
            for k in range(1, chips):
                summed = summed + in_first[h, k - 1].astype(f32)
            parts = [(everything, summed)]
        if h == 0:
            momentum_copy.wait()
        here = pl.ds(h * STEP, STEP)
        for cols, summed in parts:
            updated = momentum_decay * momentum[here, cols] + summed
            new_momentum[here, cols] = updated
            blended = summed + momentum_decay * updated
            columns[rows_of(h, d), cols] = blended.astype(bf16)
            square_sum.append(jnp.sum(blended * blended))
        mine = columns.at[rows_of(h, d)]
        for k in range(1, 3 if square_plane else chips):
            send(mine, mine, 3, gather_sem.at[h], device_at(k))
        send(mine, mine, 5, core_sem.at[h], partner)

    def pass_on(h):
        near = range(1, 3 if square_plane else chips)
        wait_for(stripes(len(near) * STEP * width), gather_sem.at[h])
        for k in near:
            there = columns.at[rows_of(h, 2 * behind[k] + core)]
            if square_plane:
                part = columns.at[
                    rows_of(h, 2 * behind[k] + core), (left, right)[k - 1]
                ]
                send(part, part, 4, relay_sem.at[h], device_at(3 - k))
            send(there, there, 5, core_sem.at[h], partner)

    def pass_diagonal(h):
        if square_plane:
            there = columns.at[rows_of(h, 2 * across + core)]
            wait_for(there, relay_sem.at[h])
            send(there, there, 5, core_sem.at[h], partner)

    def part_gram(piece):
        h, low, high = pieces[piece]
        if high == h + 1:
            wait_for(stripes(chips * STEP * width), core_sem.at[h])
        own_gram[piece] = lax.dot_general(
            columns[rows_of(h, d)],
            columns[low * block : high * block],
            (((1,), (1,)), ((), ())),
            preferred_element_type=f32,
        )
        reach = pl.ds(low * block, (high - low) * block)
        gram_own[h, :, reach] = own_gram[piece].astype(bf16)
        for k in range(1, fsdp_count):
            send(
                gram_own.at[h, :, reach],
                gram_in.at[h, k - 1, :, reach],
                6,
                gram_wide_sem.at[piece],
                (d, lax.rem(f + k, fsdp_count)),
            )

    def whole_gram(piece):
        h, low, high = pieces[piece]
        reach = pl.ds(low * block, (high - low) * block)
        total = own_gram[piece]
        wait_for(gram_in.at[h, :, :, reach], gram_wide_sem.at[piece])
        for k in range(1, fsdp_count):
            total = total + gram_in[h, k - 1, :, reach].astype(f32)
        gram[rows_of(h, d), reach] = total.astype(bf16)
        mine = gram.at[rows_of(h, d), reach]
        for k in range(1, dp_count):
            send(mine, mine, 7, last_sem.at[0], (lax.rem(d + k, dp_count), f))

    corner = pl.ds((steps - 1) * block, block)
    corner_total = {}
    middle = block // 2
    quarter = block // 4

    def part_corner():
        wait_for(stripes(chips * STEP * width), core_sem.at[steps - 1])
        newest = columns[corner]
        full = lax.dot_general(
            newest, newest, (((1,), (1,)), ((), ())), preferred_element_type=f32
        )
        packed = jnp.concatenate(
            [
                full[middle:block],
                jnp.concatenate([full[0:quarter, 0:middle], full[quarter:middle, 0:middle]], axis=1),
            ],
            axis=0,
        )
        corner_total[0] = packed
        corner_own[...] = packed.astype(bf16)
        for k in range(1, fsdp_count):
            send(
                corner_own,
                corner_in.at[k - 1],
                10,
                last_sem.at[3],
                (d, lax.rem(f + k, fsdp_count)),
            )

    def whole_corner():
        wait_for(corner_in, last_sem.at[3])
        total = corner_total[0]
        for k in range(1, fsdp_count):
            total = total + corner_in[k - 1].astype(f32)
        total = total.astype(bf16).astype(f32)
        first_half = jnp.concatenate(
            [total[middle:, 0:middle], total[middle:, middle:block]], axis=0
        )
        first_half = jnp.concatenate([first_half, jnp.zeros_like(first_half)], axis=1)
        gram[pl.ds(corner.start, middle), corner] = first_half.astype(bf16)
        gram[pl.ds(corner.start + middle, middle), corner] = total[0:middle].astype(bf16)

    def stats_send():
        total = square_sum[0]
        for value in square_sum[1:]:
            total = total + value
        peaks_copy.wait()
        stats_in[d] = jnp.full((8, 128), total, f32)
        stats_in[d, 0:1, 0:HEADS] = peaks[...].astype(f32)
        for k in range(1, dp_count):
            send(
                stats_in.at[d, pl.ds(0, 2)],
                stats_in.at[d, pl.ds(0, 2)],
                8,
                last_sem.at[1],
                (lax.rem(d + k, dp_count), f),
            )

    def stats_pass():
        wait_for(stats_in.at[pl.ds(0, dp_count - 1), pl.ds(0, 2)], last_sem.at[1])
        stats_wide[f, 0:1] = functools.reduce(
            jnp.maximum, [stats_in[j, 0:1] for j in range(dp_count)]
        )
        stats_wide[f, 1:2] = sum(stats_in[j, 1:2] for j in range(dp_count))
        for k in range(1, fsdp_count):
            send(
                stats_wide.at[f, pl.ds(0, 2)],
                stats_wide.at[f, pl.ds(0, 2)],
                9,
                last_sem.at[2],
                (d, lax.rem(f + k, fsdp_count)),
            )

    def stats_end():
        wait_for(stats_wide.at[pl.ds(0, fsdp_count - 1), pl.ds(0, 2)], last_sem.at[2])
        stats_out[0:1] = functools.reduce(
            jnp.maximum, [stats_wide[j, 0:1] for j in range(fsdp_count)]
        )
        stats_out[1:2] = sum(stats_wide[j, 1:2] for j in range(fsdp_count))

    acts = {
        "F": first_send,
        "S": second_send,
        "B": blend,
        "P": pass_on,
        "D": pass_diagonal,
        "G": part_gram,
        "Z": whole_gram,
        "C": part_corner,
        "E": whole_corner,
        "T": stats_send,
        "U": stats_pass,
    }
    for act in order_of(steps):
        acts[act[0]](*(int(digit) for digit in act[1:]))
    stats_end()
    wait_for(stripes(volume[7]), last_sem.at[0])
    if volume[10]:
        wait_for(corner_in, sent_sem.at[10])
    for sender in range(8):
        if volume[sender]:
            wait_for(stripes(volume[sender]), sent_sem.at[sender])
    wait_for(stats_in.at[pl.ds(0, dp_count - 1), pl.ds(0, 2)], sent_sem.at[8])
    wait_for(stats_wide.at[pl.ds(0, fsdp_count - 1), pl.ds(0, 2)], sent_sem.at[9])


def reduce_and_gather(gradient, momentum, peaks):
    dp_count = lax.axis_size("dp")
    fsdp_count = lax.axis_size("fsdp")
    chips = dp_count // 2
    rows, width = momentum.shape
    steps = rows // STEP
    half = width // 2
    square_plane = chips == 4
    gradient = gradient.reshape(chips, 2, steps, STEP, width)
    in_hbm = pl.BlockSpec(memory_space=pltpu.HBM)
    in_vmem = pl.BlockSpec(memory_space=pltpu.VMEM)
    if square_plane:
        first = (steps, 2, 2, STEP, half)
        second = (steps, 2, STEP, half)
    else:
        first = (steps, chips - 1, STEP, width)
        second = (1, 1, STEP, 128)
    dma = pltpu.SemaphoreType.DMA
    return pl.pallas_call(
        functools.partial(exchange, dp_count, fsdp_count),
        out_shape=(
            pltpu.VMEM((rows, width), f32),
            pltpu.VMEM((KVL, width), bf16),
            pltpu.VMEM((KVL, KVL), bf16),
            pltpu.VMEM((8, 128), f32),
        ),
        in_specs=[in_hbm] * 3,
        out_specs=(in_vmem,) * 4,
        scratch_shapes=[
            pltpu.VMEM((steps, chips, STEP, width), bf16),
            pltpu.VMEM((steps, chips, STEP, width), bf16),
            pltpu.VMEM((rows, width), f32),
            pltpu.VMEM((1, HEADS), jnp.int32),
            pltpu.VMEM(first, bf16),
            pltpu.VMEM(first, bf16),
            pltpu.VMEM(second, bf16),
            pltpu.VMEM(second, bf16),
            pltpu.VMEM((steps, STEP, KVL), bf16),
            pltpu.VMEM((steps, fsdp_count - 1, STEP, KVL), bf16),
            pltpu.VMEM((dp_count, 8, 128), f32),
            pltpu.VMEM((fsdp_count, 8, 128), f32),
            dma((steps + 2,)),
            dma((SENDERS,)),
            dma((steps,)),
            dma((steps,)),
            dma((steps,)),
            dma((steps,)),
            dma((steps,)),
            dma((steps,)),
            dma((len(pieces_of(steps)),)),
            dma((4,)),
            pltpu.VMEM((dp_count * STEP * 3 // 4, dp_count * STEP), bf16),
            pltpu.VMEM((fsdp_count - 1, dp_count * STEP * 3 // 4, dp_count * STEP), bf16),
        ],
        compiler_params=pltpu.CompilerParams(
            collective_id=0, has_side_effects=True, vmem_limit_bytes=24 * 1024 * 1024
        ),
        cost_estimate=pl.CostEstimate(
            flops=40_000_000_000, bytes_accessed=4_000_000, transcendentals=0
        ),
    )(*(pltpu.with_memory_space_constraint(x, pltpu.HBM) for x in (gradient, momentum, peaks)))


def product(left, right):
    return jnp.dot(left.astype(bf16), right.astype(bf16), preferred_element_type=f32)


def finish(
    dp_count,
    new_momentum,
    columns,
    gram,
    stats,
    weight,
    clip,
    new_weight_all,
    new_momentum_all,
    update_norm,
    new_weight,
    full_gram,
    small_sem,
    out_sem,
):
    rows, width = new_momentum.shape
    steps = rows // STEP
    span = NOPE + VDIM
    heads = width // span
    lead, second, third = quintic_terms
    momentum_copy = pltpu.make_async_copy(new_momentum, new_momentum_all, small_sem.at[0])
    momentum_copy.start()

    block = dp_count * STEP
    for i in range(steps):
        reach = (i + 1) * block
        full_gram[i * block : reach, 0:reach] = gram[i * block : reach, 0:reach]
        if i and i == steps - 1:
            middle = reach - block // 2
            piece = gram[middle:reach, i * block : middle].astype(f32)
            full_gram[i * block : middle, middle:reach] = piece.T.astype(bf16)
        for j in range(i):
            piece = gram[i * block : reach, j * block : (j + 1) * block].astype(f32)
            full_gram[j * block : (j + 1) * block, i * block : reach] = piece.T.astype(bf16)

    level = stats[1:2, 0:1]
    update_norm[0] = jnp.sqrt(level * (1.0 / (KVL * KVO)))[0, 0]
    inverse = 1.0 / (jnp.sqrt(level) + epsilon)
    scale = inverse * inverse
    total = full_gram[...]
    gram_now = total.astype(f32) * scale
    square = (scale * scale) * jnp.dot(total, total, preferred_element_type=f32)
    rest = second * gram_now + third * square
    beyond = rest
    part = lead * gram_now + scale * jnp.dot(
        rest.astype(bf16), total, preferred_element_type=f32
    )
    for iteration in range(1, ITERS):
        gram_now = lead * part + product(part, rest)
        rest = second * gram_now + third * product(gram_now, gram_now)
        beyond = lead * beyond + lead**iteration * rest + product(rest, beyond)
        if iteration < ITERS - 1:
            part = lead * gram_now + product(rest, gram_now)
    row = lax.broadcasted_iota(jnp.int32, (KVL, KVL), 0)
    col = lax.broadcasted_iota(jnp.int32, (KVL, KVL), 1)
    whole = jnp.where(row == col, beyond + lead**ITERS, beyond).astype(bf16)

    threshold = clip[0].astype(f32)
    factors = jnp.sqrt(jnp.minimum(1.0, threshold / stats[0:1]))
    lane = lax.broadcasted_iota(jnp.int32, (1, 128), 1)
    first_head = lax.axis_index("fsdp") * heads
    update_scale = (learning_rate * update_gain * math.sqrt(max(KVL, KVO))) * inverse
    factor_row = jnp.concatenate(
        [
            piece
            for j in range(heads)
            for piece in (
                jnp.broadcast_to(
                    jnp.sum(
                        jnp.where(lane == first_head + j, factors, 0.0), axis=1, keepdims=True
                    ),
                    (1, NOPE),
                ),
                jnp.ones((1, VDIM), f32),
            )
        ],
        axis=1,
    )
    keep = factor_row * (1.0 - learning_rate * weight_decay)
    move = factor_row * update_scale
    out_copies = []
    group = min(GROUP, steps)
    for g in range(steps // group):
        rows_now = whole[g * group * block : (g + 1) * group * block]
        for j in range(width // span):
            cols = pl.ds(j * span, span)
            orthogonal = jnp.dot(rows_now, columns[:, cols], preferred_element_type=f32)
            for i in range(group):
                h = g * group + i
                for device in range(dp_count):
                    start = (i * dp_count + device) * STEP
                    new_weight[device, h, :, cols] = (
                        keep[:, j * span : (j + 1) * span] * weight[device, h, :, cols]
                        - move[:, j * span : (j + 1) * span] * orthogonal[start : start + STEP]
                    )
        here = pl.ds(g * group, group)
        copy = pltpu.make_async_copy(
            new_weight.at[:, here], new_weight_all.at[:, here], out_sem.at[g]
        )
        copy.start()
        out_copies.append(copy)
    momentum_copy.wait()
    for copy in out_copies:
        copy.wait()


def polish(new_momentum, columns, gram, stats, weight, clip_threshold):
    dp_count = lax.axis_size("dp")
    rows, width = new_momentum.shape
    steps = rows // STEP
    in_hbm = pl.BlockSpec(memory_space=pltpu.HBM)
    in_vmem = pl.BlockSpec(memory_space=pltpu.VMEM)
    dma = pltpu.SemaphoreType.DMA
    weight = weight.reshape(dp_count, steps, STEP, width)
    new_weight, new_momentum, update_norm = pl.pallas_call(
        functools.partial(finish, dp_count),
        out_shape=(
            jax.ShapeDtypeStruct((dp_count, steps, STEP, width), f32),
            jax.ShapeDtypeStruct((rows, width), f32),
            jax.ShapeDtypeStruct((1,), f32),
        ),
        in_specs=[in_vmem] * 5 + [pl.BlockSpec(memory_space=pltpu.SMEM)],
        out_specs=(in_hbm, in_hbm, pl.BlockSpec(memory_space=pltpu.SMEM)),
        scratch_shapes=[
            pltpu.VMEM((dp_count, steps, STEP, width), f32),
            pltpu.VMEM((KVL, KVL), bf16),
            dma((1,)),
            dma((steps,)),
        ],
        compiler_params=pltpu.CompilerParams(vmem_limit_bytes=24 * 1024 * 1024),
    )(new_momentum, columns, gram, stats, weight, clip_threshold)
    return new_weight.reshape(KVL, width), new_momentum, update_norm


def local(gradients, momentum, weight, logit_peaks, clip_threshold):
    exchanged = reduce_and_gather(gradients, momentum, logit_peaks)
    return polish(*exchanged, weight, clip_threshold)


def solution(mesh):
    placed = (P("dp", None, "fsdp"), P("dp", "fsdp"), P(None, "fsdp"), P(("dp", "fsdp"), None), P())
    return jax.shard_map(
        local,
        mesh=mesh,
        in_specs=placed,
        out_specs=(P(None, "fsdp"), P("dp", "fsdp"), P()),
        check_vma=False,
    )
```

```python
import functools
import math

import jax
import jax.numpy as jnp
from jax import lax
from jax.experimental import pallas as pl
from jax.experimental.pallas import tpu as pltpu
from jax.sharding import PartitionSpec as P

KVL = 512
NOPE = 128
VDIM = 128
HEADS = 32
ITERS = 3
KVO = 8192


quintic_terms = (3.4445, -4.775, 2.0315)
learning_rate = 0.5
weight_decay = 0.1
momentum_decay = 0.95
update_gain = 0.2
epsilon = 1e-07

STEP = 16
SENDERS = 11
GROUP = 1
ORDER = (
    "F0 F1 F2 F3",
    "S0 S1 S2 S3",
    "B0 B1 B2 P0",
    "B3 T P1 P2",
    "D0 P3 D1 G0",
    "D2 G1 G2 D3",
    "C U Z0 Z1",
    "Z2 E",
)
MESH = pl.DeviceIdType.MESH
f32 = jnp.float32
bf16 = jnp.bfloat16


def pieces_of(steps):
    if steps == 1:
        return [(0, 1, 1)]
    return [(h, h + 1, h + 1) for h in range(steps - 2)] + [(steps - 2, steps, steps - 1)]


def order_of(steps):
    assert steps in (1, 4)
    if steps == 4:
        return " ".join(ORDER).split()
    last = len(pieces_of(steps))
    stages = [[kind + str(h) for h in range(steps)] for kind in "FSBPD"]
    grams = [[kind + str(piece) for piece in range(last)] for kind in "GZ"]
    return sum(stages[:3], []) + ["T"] + sum(stages[3:], []) + ["U"] + sum(grams, [])


def exchange(
    dp_count,
    fsdp_count,
    grad_all,
    momentum_all,
    peaks_all,
    new_momentum,
    columns,
    gram,
    stats_out,
    kept,
    pair,
    momentum,
    peaks,
    out_first,
    in_first,
    out_second,
    in_second,
    gram_own,
    gram_in,
    stats_in,
    stats_wide,
    local_sem,
    sent_sem,
    pair_sem,
    first_sem,
    second_sem,
    gather_sem,
    relay_sem,
    core_sem,
    gram_wide_sem,
    last_sem,
    corner_own,
    corner_in,
):
    d = lax.axis_index("dp")
    f = lax.axis_index("fsdp")
    chips = dp_count // 2
    q = d // 2
    core = d % 2
    steps = kept.shape[0]
    width = momentum.shape[1]
    half = width // 2
    left = pl.ds(0, half)
    right = pl.ds(half, half)
    square_plane = chips == 4
    partner = (2 * q + 1 - core, f)

    barrier = pltpu.get_barrier_semaphore()
    for k in range(1, dp_count):
        pl.semaphore_signal(
            barrier, inc=1, device_id=(lax.rem(d + k, dp_count), f), device_id_type=MESH
        )
    for k in range(1, fsdp_count):
        pl.semaphore_signal(
            barrier, inc=1, device_id=(d, lax.rem(f + k, fsdp_count)), device_id_type=MESH
        )
    kept_copies = [
        pltpu.make_async_copy(grad_all.at[:, core, h], kept.at[h], local_sem.at[h])
        for h in range(steps)
    ]
    momentum_copy = pltpu.make_async_copy(momentum_all, momentum, local_sem.at[steps])
    peaks_copy = pltpu.make_async_copy(peaks_all, peaks, local_sem.at[steps + 1])
    for copy in kept_copies + [momentum_copy, peaks_copy]:
        copy.start()
    pl.semaphore_wait(barrier, dp_count + fsdp_count - 2)

    volume = [0] * SENDERS

    def send(source, target, sender, arrival, device):
        volume[sender] += math.prod(source.shape)
        pltpu.make_async_remote_copy(
            src_ref=source,
            dst_ref=target,
            send_sem=sent_sem.at[sender],
            recv_sem=arrival,
            device_id=device,
            device_id_type=MESH,
        ).start()

    def wait_for(like, arrival):
        pltpu.make_async_copy(like, like, arrival).wait()

    def stripes(count):
        lanes = count // STEP
        cols = max(c for c in range(128, width + 1, 128) if lanes % c == 0)
        return columns.at[pl.ds(0, lanes // cols * STEP), pl.ds(0, cols)]

    if square_plane:
        flat, upright, across = q + 1 - 2 * (q % 2), q + 2 - 4 * (q // 2), 3 - q
        ahead = (q, flat, upright, across)
        behind = ahead
    else:
        ahead = tuple(lax.rem(q + k, chips) for k in range(chips))
        behind = tuple(lax.rem(q + chips - k, chips) for k in range(chips))

    def device_at(k):
        return (2 * ahead[k] + core, f)

    def mine_of(h, chip, cols):
        return kept[h, chip, :, cols].astype(f32) + pair[h, chip, :, cols].astype(f32)

    def rows_of(h, device):
        return pl.ds(pl.multiple_of((h * dp_count + device) * STEP, STEP), STEP)

    for h in range(steps):
        send(grad_all.at[:, 1 - core, h], pair.at[h], 0, pair_sem.at[h], partner)
    everything = pl.ds(0, width)
    own_gram = {}
    block = dp_count * STEP
    pieces = pieces_of(steps)
    square_sum = []

    def first_send(h):
        kept_copies[h].wait()
        wait_for(pair.at[h], pair_sem.at[h])
        if square_plane:
            for side, (k, cols) in enumerate(((1, left), (2, right))):
                for j, chip in enumerate((ahead[k], ahead[3])):
                    out_first[h, side, j] = mine_of(h, chip, cols).astype(bf16)
                send(
                    out_first.at[h, side],
                    in_first.at[h, side],
                    1,
                    first_sem.at[h],
                    device_at(k),
                )
        else:
            for k in range(1, chips):
                out_first[h, k - 1] = mine_of(h, ahead[k], everything).astype(bf16)
                send(
                    out_first.at[h, k - 1],
                    in_first.at[h, k - 1],
                    1,
                    first_sem.at[h],
                    device_at(k),
                )

    def second_send(h):
        wait_for(in_first.at[h], first_sem.at[h])
        if square_plane:
            for side, (k, cols) in enumerate(((2, left), (1, right))):
                out_second[h, side] = (
                    mine_of(h, ahead[k], cols) + in_first[h, side, 1].astype(f32)
                ).astype(bf16)
                send(
                    out_second.at[h, side],
                    in_second.at[h, side],
                    2,
                    second_sem.at[h],
                    device_at(k),
                )

    def blend(h):
        if square_plane:
            parts = []
            wait_for(in_second.at[h], second_sem.at[h])
            for side, cols in enumerate((left, right)):
                parts.append(
                    (
                        cols,
                        mine_of(h, q, cols)
                        + in_first[h, side, 0].astype(f32)
                        + in_second[h, side].astype(f32),
                    )
                )
        else:
            summed = mine_of(h, q, everything)
            for k in range(1, chips):
                summed = summed + in_first[h, k - 1].astype(f32)
            parts = [(everything, summed)]
        if h == 0:
            momentum_copy.wait()
        here = pl.ds(h * STEP, STEP)
        for cols, summed in parts:
            updated = momentum_decay * momentum[here, cols] + summed
            new_momentum[here, cols] = updated
            blended = summed + momentum_decay * updated
            columns[rows_of(h, d), cols] = blended.astype(bf16)
            square_sum.append(jnp.sum(blended * blended))
        mine = columns.at[rows_of(h, d)]
        for k in range(1, 3 if square_plane else chips):
            send(mine, mine, 3, gather_sem.at[h], device_at(k))
        send(mine, mine, 5, core_sem.at[h], partner)

    def pass_on(h):
        near = range(1, 3 if square_plane else chips)
        wait_for(stripes(len(near) * STEP * width), gather_sem.at[h])
        for k in near:
            there = columns.at[rows_of(h, 2 * behind[k] + core)]
            if square_plane:
                part = columns.at[
                    rows_of(h, 2 * behind[k] + core), (left, right)[k - 1]
                ]
                send(part, part, 4, relay_sem.at[h], device_at(3 - k))
            send(there, there, 5, core_sem.at[h], partner)

    def pass_diagonal(h):
        if square_plane:
            there = columns.at[rows_of(h, 2 * across + core)]
            wait_for(there, relay_sem.at[h])
            send(there, there, 5, core_sem.at[h], partner)

    def part_gram(piece):
        low, high, reach = pieces[piece]
        wait_for(stripes(chips * STEP * width), core_sem.at[reach - 1])
        mine = [columns[rows_of(h, d)] for h in range(low, high)]
        own_gram[piece] = lax.dot_general(
            mine[0] if len(mine) == 1 else jnp.concatenate(mine, axis=0),
            columns[0 : reach * block],
            (((1,), (1,)), ((), ())),
            preferred_element_type=f32,
        )
        cols = pl.ds(0, reach * block)
        for h in range(low, high):
            gram_own[h, :, cols] = own_gram[piece][
                (h - low) * STEP : (h - low + 1) * STEP
            ].astype(bf16)
        steps_now = pl.ds(low, high - low)
        for k in range(1, fsdp_count):
            send(
                gram_own.at[steps_now, :, cols],
                gram_in.at[k - 1, steps_now, :, cols],
                6,
                gram_wide_sem.at[piece],
                (d, lax.rem(f + k, fsdp_count)),
            )

    def whole_gram(piece):
        low, high, reach = pieces[piece]
        cols = pl.ds(0, reach * block)
        steps_now = pl.ds(low, high - low)
        here = pl.ds(pl.multiple_of(d * STEP, STEP), STEP)
        wait_for(gram_in.at[:, steps_now, :, cols], gram_wide_sem.at[piece])
        for h in range(low, high):
            total = own_gram[piece][(h - low) * STEP : (h - low + 1) * STEP]
            for k in range(1, fsdp_count):
                total = total + gram_in[k - 1, h, :, cols].astype(f32)
            gram[h, here, cols] = total.astype(bf16)
        mine = gram.at[steps_now, here, cols]
        for k in range(1, dp_count):
            send(mine, mine, 7, last_sem.at[0], (lax.rem(d + k, dp_count), f))

    corner = pl.ds((steps - 1) * block, block)
    corner_total = {}
    middle = block // 2
    quarter = block // 4

    def part_corner():
        wait_for(stripes(chips * STEP * width), core_sem.at[steps - 1])
        newest = columns[corner]
        full = lax.dot_general(
            newest, newest, (((1,), (1,)), ((), ())), preferred_element_type=f32
        )
        packed = jnp.concatenate(
            [
                full[middle:block],
                jnp.concatenate([full[0:quarter, 0:middle], full[quarter:middle, 0:middle]], axis=1),
            ],
            axis=0,
        )
        corner_total[0] = packed
        corner_own[...] = packed.astype(bf16)
        for k in range(1, fsdp_count):
            send(
                corner_own,
                corner_in.at[k - 1],
                10,
                last_sem.at[3],
                (d, lax.rem(f + k, fsdp_count)),
            )

    def whole_corner():
        wait_for(corner_in, last_sem.at[3])
        total = corner_total[0]
        for k in range(1, fsdp_count):
            total = total + corner_in[k - 1].astype(f32)
        total = total.astype(bf16).astype(f32)
        first_half = jnp.concatenate(
            [total[middle:, 0:middle], total[middle:, middle:block]], axis=0
        )
        first_half = jnp.concatenate([first_half, jnp.zeros_like(first_half)], axis=1)
        gram[steps - 1, pl.ds(0, middle), corner] = first_half.astype(bf16)
        gram[steps - 1, pl.ds(middle, middle), corner] = total[0:middle].astype(bf16)

    def stats_send():
        total = square_sum[0]
        for value in square_sum[1:]:
            total = total + value
        peaks_copy.wait()
        stats_in[d] = jnp.full((8, 128), total, f32)
        stats_in[d, 0:1, 0:HEADS] = peaks[...].astype(f32)
        for k in range(1, dp_count):
            send(
                stats_in.at[d, pl.ds(0, 2)],
                stats_in.at[d, pl.ds(0, 2)],
                8,
                last_sem.at[1],
                (lax.rem(d + k, dp_count), f),
            )

    def stats_pass():
        wait_for(stats_in.at[pl.ds(0, dp_count - 1), pl.ds(0, 2)], last_sem.at[1])
        stats_wide[f, 0:1] = functools.reduce(
            jnp.maximum, [stats_in[j, 0:1] for j in range(dp_count)]
        )
        stats_wide[f, 1:2] = sum(stats_in[j, 1:2] for j in range(dp_count))
        for k in range(1, fsdp_count):
            send(
                stats_wide.at[f, pl.ds(0, 2)],
                stats_wide.at[f, pl.ds(0, 2)],
                9,
                last_sem.at[2],
                (d, lax.rem(f + k, fsdp_count)),
            )

    def stats_end():
        wait_for(stats_wide.at[pl.ds(0, fsdp_count - 1), pl.ds(0, 2)], last_sem.at[2])
        stats_out[0:1] = functools.reduce(
            jnp.maximum, [stats_wide[j, 0:1] for j in range(fsdp_count)]
        )
        stats_out[1:2] = sum(stats_wide[j, 1:2] for j in range(fsdp_count))

    acts = {
        "F": first_send,
        "S": second_send,
        "B": blend,
        "P": pass_on,
        "D": pass_diagonal,
        "G": part_gram,
        "Z": whole_gram,
        "C": part_corner,
        "E": whole_corner,
        "T": stats_send,
        "U": stats_pass,
    }
    for act in order_of(steps):
        acts[act[0]](*(int(digit) for digit in act[1:]))
    stats_end()
    wait_for(stripes(volume[7]), last_sem.at[0])
    if volume[10]:
        wait_for(corner_in, sent_sem.at[10])
    for sender in range(8):
        if volume[sender]:
            wait_for(stripes(volume[sender]), sent_sem.at[sender])
    wait_for(stats_in.at[pl.ds(0, dp_count - 1), pl.ds(0, 2)], sent_sem.at[8])
    wait_for(stats_wide.at[pl.ds(0, fsdp_count - 1), pl.ds(0, 2)], sent_sem.at[9])


def reduce_and_gather(gradient, momentum, peaks):
    dp_count = lax.axis_size("dp")
    fsdp_count = lax.axis_size("fsdp")
    chips = dp_count // 2
    rows, width = momentum.shape
    steps = rows // STEP
    half = width // 2
    square_plane = chips == 4
    gradient = gradient.reshape(chips, 2, steps, STEP, width)
    in_hbm = pl.BlockSpec(memory_space=pltpu.HBM)
    in_vmem = pl.BlockSpec(memory_space=pltpu.VMEM)
    if square_plane:
        first = (steps, 2, 2, STEP, half)
        second = (steps, 2, STEP, half)
    else:
        first = (steps, chips - 1, STEP, width)
        second = (1, 1, STEP, 128)
    dma = pltpu.SemaphoreType.DMA
    return pl.pallas_call(
        functools.partial(exchange, dp_count, fsdp_count),
        out_shape=(
            pltpu.VMEM((rows, width), f32),
            pltpu.VMEM((KVL, width), bf16),
            pltpu.VMEM((steps, dp_count * STEP, KVL), bf16),
            pltpu.VMEM((8, 128), f32),
        ),
        in_specs=[in_hbm] * 3,
        out_specs=(in_vmem,) * 4,
        scratch_shapes=[
            pltpu.VMEM((steps, chips, STEP, width), bf16),
            pltpu.VMEM((steps, chips, STEP, width), bf16),
            pltpu.VMEM((rows, width), f32),
            pltpu.VMEM((1, HEADS), jnp.int32),
            pltpu.VMEM(first, bf16),
            pltpu.VMEM(first, bf16),
            pltpu.VMEM(second, bf16),
            pltpu.VMEM(second, bf16),
            pltpu.VMEM((steps, STEP, KVL), bf16),
            pltpu.VMEM((fsdp_count - 1, steps, STEP, KVL), bf16),
            pltpu.VMEM((dp_count, 8, 128), f32),
            pltpu.VMEM((fsdp_count, 8, 128), f32),
            dma((steps + 2,)),
            dma((SENDERS,)),
            dma((steps,)),
            dma((steps,)),
            dma((steps,)),
            dma((steps,)),
            dma((steps,)),
            dma((steps,)),
            dma((len(pieces_of(steps)),)),
            dma((4,)),
            pltpu.VMEM((dp_count * STEP * 3 // 4, dp_count * STEP), bf16),
            pltpu.VMEM((fsdp_count - 1, dp_count * STEP * 3 // 4, dp_count * STEP), bf16),
        ],
        compiler_params=pltpu.CompilerParams(
            collective_id=0, has_side_effects=True, vmem_limit_bytes=24 * 1024 * 1024
        ),
        cost_estimate=pl.CostEstimate(
            flops=40_000_000_000, bytes_accessed=4_000_000, transcendentals=0
        ),
    )(*(pltpu.with_memory_space_constraint(x, pltpu.HBM) for x in (gradient, momentum, peaks)))


def product(left, right):
    return jnp.dot(left.astype(bf16), right.astype(bf16), preferred_element_type=f32)


def finish(
    dp_count,
    new_momentum,
    columns,
    gram,
    stats,
    weight,
    clip,
    new_weight_all,
    new_momentum_all,
    update_norm,
    new_weight,
    full_gram,
    small_sem,
    out_sem,
):
    rows, width = new_momentum.shape
    steps = rows // STEP
    span = NOPE + VDIM
    heads = width // span
    lead, second, third = quintic_terms
    momentum_copy = pltpu.make_async_copy(new_momentum, new_momentum_all, small_sem.at[0])
    momentum_copy.start()

    block = dp_count * STEP
    for i in range(steps):
        reach = (i + 1) * block
        full_gram[i * block : reach, 0:reach] = gram[i, :, 0:reach]
        if i and i == steps - 1:
            middle = reach - block // 2
            piece = gram[i, block // 2 : block, i * block : middle].astype(f32)
            full_gram[i * block : middle, middle:reach] = piece.T.astype(bf16)
        for j in range(i):
            piece = gram[i, :, j * block : (j + 1) * block].astype(f32)
            full_gram[j * block : (j + 1) * block, i * block : reach] = piece.T.astype(bf16)

    level = stats[1:2, 0:1]
    update_norm[0] = jnp.sqrt(level * (1.0 / (KVL * KVO)))[0, 0]
    inverse = 1.0 / (jnp.sqrt(level) + epsilon)
    scale = inverse * inverse
    total = full_gram[...]
    gram_now = total.astype(f32) * scale
    square = (scale * scale) * jnp.dot(total, total, preferred_element_type=f32)
    rest = second * gram_now + third * square
    beyond = rest
    part = lead * gram_now + scale * jnp.dot(
        rest.astype(bf16), total, preferred_element_type=f32
    )
    for iteration in range(1, ITERS):
        gram_now = lead * part + product(part, rest)
        rest = second * gram_now + third * product(gram_now, gram_now)
        beyond = lead * beyond + lead**iteration * rest + product(rest, beyond)
        if iteration < ITERS - 1:
            part = lead * gram_now + product(rest, gram_now)
    row = lax.broadcasted_iota(jnp.int32, (KVL, KVL), 0)
    col = lax.broadcasted_iota(jnp.int32, (KVL, KVL), 1)
    whole = jnp.where(row == col, beyond + lead**ITERS, beyond).astype(bf16)

    threshold = clip[0].astype(f32)
    factors = jnp.sqrt(jnp.minimum(1.0, threshold / stats[0:1]))
    lane = lax.broadcasted_iota(jnp.int32, (1, 128), 1)
    first_head = lax.axis_index("fsdp") * heads
    update_scale = (learning_rate * update_gain * math.sqrt(max(KVL, KVO))) * inverse
    factor_row = jnp.concatenate(
        [
            piece
            for j in range(heads)
            for piece in (
                jnp.broadcast_to(
                    jnp.sum(
                        jnp.where(lane == first_head + j, factors, 0.0), axis=1, keepdims=True
                    ),
                    (1, NOPE),
                ),
                jnp.ones((1, VDIM), f32),
            )
        ],
        axis=1,
    )
    keep = factor_row * (1.0 - learning_rate * weight_decay)
    move = factor_row * update_scale
    out_copies = []
    group = min(GROUP, steps)
    for g in range(steps // group):
        rows_now = whole[g * group * block : (g + 1) * group * block]
        for j in range(width // span):
            cols = pl.ds(j * span, span)
            orthogonal = jnp.dot(rows_now, columns[:, cols], preferred_element_type=f32)
            for i in range(group):
                h = g * group + i
                for device in range(dp_count):
                    start = (i * dp_count + device) * STEP
                    new_weight[device, h, :, cols] = (
                        keep[:, j * span : (j + 1) * span] * weight[device, h, :, cols]
                        - move[:, j * span : (j + 1) * span] * orthogonal[start : start + STEP]
                    )
        here = pl.ds(g * group, group)
        copy = pltpu.make_async_copy(
            new_weight.at[:, here], new_weight_all.at[:, here], out_sem.at[g]
        )
        copy.start()
        out_copies.append(copy)
    momentum_copy.wait()
    for copy in out_copies:
        copy.wait()


def polish(new_momentum, columns, gram, stats, weight, clip_threshold):
    dp_count = lax.axis_size("dp")
    rows, width = new_momentum.shape
    steps = rows // STEP
    in_hbm = pl.BlockSpec(memory_space=pltpu.HBM)
    in_vmem = pl.BlockSpec(memory_space=pltpu.VMEM)
    dma = pltpu.SemaphoreType.DMA
    weight = weight.reshape(dp_count, steps, STEP, width)
    new_weight, new_momentum, update_norm = pl.pallas_call(
        functools.partial(finish, dp_count),
        out_shape=(
            jax.ShapeDtypeStruct((dp_count, steps, STEP, width), f32),
            jax.ShapeDtypeStruct((rows, width), f32),
            jax.ShapeDtypeStruct((1,), f32),
        ),
        in_specs=[in_vmem] * 5 + [pl.BlockSpec(memory_space=pltpu.SMEM)],
        out_specs=(in_hbm, in_hbm, pl.BlockSpec(memory_space=pltpu.SMEM)),
        scratch_shapes=[
            pltpu.VMEM((dp_count, steps, STEP, width), f32),
            pltpu.VMEM((KVL, KVL), bf16),
            dma((1,)),
            dma((steps,)),
        ],
        compiler_params=pltpu.CompilerParams(vmem_limit_bytes=24 * 1024 * 1024),
    )(new_momentum, columns, gram, stats, weight, clip_threshold)
    return new_weight.reshape(KVL, width), new_momentum, update_norm


def local(gradients, momentum, weight, logit_peaks, clip_threshold):
    exchanged = reduce_and_gather(gradients, momentum, logit_peaks)
    return polish(*exchanged, weight, clip_threshold)


def solution(mesh):
    placed = (P("dp", None, "fsdp"), P("dp", "fsdp"), P(None, "fsdp"), P(("dp", "fsdp"), None), P())
    return jax.shard_map(
        local,
        mesh=mesh,
        in_specs=placed,
        out_specs=(P(None, "fsdp"), P("dp", "fsdp"), P()),
        check_vma=False,
    )
```

```python
import functools
import math

import jax
import jax.numpy as jnp
from jax import lax
from jax.experimental import pallas as pl
from jax.experimental.pallas import tpu as pltpu
from jax.sharding import PartitionSpec as P

KVL = 512
NOPE = 128
VDIM = 128
HEADS = 32
ITERS = 3
KVO = 8192


quintic_terms = (3.4445, -4.775, 2.0315)
learning_rate = 0.5
weight_decay = 0.1
momentum_decay = 0.95
update_gain = 0.2
epsilon = 1e-07

STEP = 16
SENDERS = 7
GROUP = 1
ORDER = (
    "F0 F1 F2 F3",
    "S0 S1 S2 S3",
    "B0 B1 B2 P0",
    "B3 T P1 P2",
    "D0 P3 D1 G0",
    "D2 G1 G2 D3",
    "C U Z0 Z1",
    "Z2 E",
)
MESH = pl.DeviceIdType.MESH
f32 = jnp.float32
bf16 = jnp.bfloat16


def pieces_of(steps):
    if steps == 1:
        return [(0, 1, 1)]
    return [(h, h + 1, h + 1) for h in range(steps - 2)] + [(steps - 2, steps, steps - 1)]


def order_of(steps):
    assert steps in (1, 4)
    if steps == 4:
        return " ".join(ORDER).split()
    last = len(pieces_of(steps))
    stages = [[kind + str(h) for h in range(steps)] for kind in "FSBPD"]
    grams = [[kind + str(piece) for piece in range(last)] for kind in "GZ"]
    return sum(stages[:3], []) + ["T"] + sum(stages[3:], []) + ["U"] + sum(grams, [])


def exchange(
    dp_count,
    fsdp_count,
    grad_all,
    momentum_all,
    peaks_all,
    new_momentum,
    columns,
    gram,
    stats_out,
    kept,
    pair,
    momentum,
    peaks,
    out_first,
    in_first,
    out_second,
    in_second,
    gram_own,
    gram_in,
    stats_in,
    stats_wide,
    local_sem,
    sent_sem,
    pair_sem,
    first_sem,
    second_sem,
    gather_sem,
    relay_sem,
    core_sem,
    gram_wide_sem,
    last_sem,
    corner_own,
    corner_in,
):
    d = lax.axis_index("dp")
    f = lax.axis_index("fsdp")
    chips = dp_count // 2
    q = d // 2
    core = d % 2
    steps = kept.shape[0]
    width = momentum.shape[1]
    half = width // 2
    left = pl.ds(0, half)
    right = pl.ds(half, half)
    square_plane = chips == 4
    partner = (2 * q + 1 - core, f)

    barrier = pltpu.get_barrier_semaphore()
    for k in range(1, dp_count):
        pl.semaphore_signal(
            barrier, inc=1, device_id=(lax.rem(d + k, dp_count), f), device_id_type=MESH
        )
    for k in range(1, fsdp_count):
        pl.semaphore_signal(
            barrier, inc=1, device_id=(d, lax.rem(f + k, fsdp_count)), device_id_type=MESH
        )
    kept_copies = [
        pltpu.make_async_copy(grad_all.at[:, core, h], kept.at[h], local_sem.at[h])
        for h in range(steps)
    ]
    momentum_copy = pltpu.make_async_copy(momentum_all, momentum, local_sem.at[steps])
    peaks_copy = pltpu.make_async_copy(peaks_all, peaks, local_sem.at[steps + 1])
    kept_copies[0].start()
    pl.semaphore_wait(barrier, dp_count + fsdp_count - 2)

    volume = [0] * SENDERS

    def send(source, target, sender, arrival, device):
        volume[sender] += math.prod(source.shape)
        pltpu.make_async_remote_copy(
            src_ref=source,
            dst_ref=target,
            send_sem=sent_sem.at[sender],
            recv_sem=arrival,
            device_id=device,
            device_id_type=MESH,
        ).start()

    def wait_for(like, arrival):
        pltpu.make_async_copy(like, like, arrival).wait()

    def stripes(count):
        lanes = count // STEP
        cols = max(c for c in range(128, width + 1, 128) if lanes % c == 0)
        return columns.at[pl.ds(0, lanes // cols * STEP), pl.ds(0, cols)]

    if square_plane:
        flat, upright, across = q + 1 - 2 * (q % 2), q + 2 - 4 * (q // 2), 3 - q
        ahead = (q, flat, upright, across)
        behind = ahead
    else:
        ahead = tuple(lax.rem(q + k, chips) for k in range(chips))
        behind = tuple(lax.rem(q + chips - k, chips) for k in range(chips))

    def device_at(k):
        return (2 * ahead[k] + core, f)

    def mine_of(h, chip, cols):
        return kept[h, chip, :, cols].astype(f32) + pair[h, chip, :, cols].astype(f32)

    def rows_of(h, device):
        return pl.ds(pl.multiple_of((h * dp_count + device) * STEP, STEP), STEP)

    for h in range(steps):
        send(grad_all.at[:, 1 - core, h], pair.at[h], 0, pair_sem.at[h], partner)
    for copy in kept_copies[1:] + [momentum_copy, peaks_copy]:
        copy.start()
    everything = pl.ds(0, width)
    own_gram = {}
    block = dp_count * STEP
    pieces = pieces_of(steps)
    square_sum = []

    def first_send(h):
        kept_copies[h].wait()
        wait_for(pair.at[h], pair_sem.at[h])
        if square_plane:
            for side, (k, cols) in enumerate(((1, left), (2, right))):
                for j, chip in enumerate((ahead[k], ahead[3])):
                    out_first[h, side, j] = mine_of(h, chip, cols).astype(bf16)
                send(
                    out_first.at[h, side],
                    in_first.at[h, side],
                    0,
                    first_sem.at[h],
                    device_at(k),
                )
        else:
            for k in range(1, chips):
                out_first[h, k - 1] = mine_of(h, ahead[k], everything).astype(bf16)
                send(
                    out_first.at[h, k - 1],
                    in_first.at[h, k - 1],
                    0,
                    first_sem.at[h],
                    device_at(k),
                )

    def second_send(h):
        wait_for(in_first.at[h], first_sem.at[h])
        if square_plane:
            for side, (k, cols) in enumerate(((2, left), (1, right))):
                out_second[h, side] = (
                    mine_of(h, ahead[k], cols) + in_first[h, side, 1].astype(f32)
                ).astype(bf16)
                send(
                    out_second.at[h, side],
                    in_second.at[h, side],
                    0,
                    second_sem.at[h],
                    device_at(k),
                )

    def blend(h):
        if square_plane:
            parts = []
            wait_for(in_second.at[h], second_sem.at[h])
            for side, cols in enumerate((left, right)):
                parts.append(
                    (
                        cols,
                        mine_of(h, q, cols)
                        + in_first[h, side, 0].astype(f32)
                        + in_second[h, side].astype(f32),
                    )
                )
        else:
            summed = mine_of(h, q, everything)
            for k in range(1, chips):
                summed = summed + in_first[h, k - 1].astype(f32)
            parts = [(everything, summed)]
        if h == 0:
            momentum_copy.wait()
        here = pl.ds(h * STEP, STEP)
        for cols, summed in parts:
            updated = momentum_decay * momentum[here, cols] + summed
            new_momentum[here, cols] = updated
            blended = summed + momentum_decay * updated
            columns[rows_of(h, d), cols] = blended.astype(bf16)
            square_sum.append(jnp.sum(blended * blended))
        mine = columns.at[rows_of(h, d)]
        for k in range(1, 3 if square_plane else chips):
            send(mine, mine, 1, gather_sem.at[h], device_at(k))
        send(mine, mine, 1, core_sem.at[h], partner)

    def pass_on(h):
        near = range(1, 3 if square_plane else chips)
        wait_for(stripes(len(near) * STEP * width), gather_sem.at[h])
        for k in near:
            there = columns.at[rows_of(h, 2 * behind[k] + core)]
            if square_plane:
                part = columns.at[
                    rows_of(h, 2 * behind[k] + core), (left, right)[k - 1]
                ]
                send(part, part, 1, relay_sem.at[h], device_at(3 - k))
            send(there, there, 1, core_sem.at[h], partner)

    def pass_diagonal(h):
        if square_plane:
            there = columns.at[rows_of(h, 2 * across + core)]
            wait_for(there, relay_sem.at[h])
            send(there, there, 1, core_sem.at[h], partner)

    def part_gram(piece):
        low, high, reach = pieces[piece]
        wait_for(stripes(chips * STEP * width), core_sem.at[reach - 1])
        mine = [columns[rows_of(h, d)] for h in range(low, high)]
        own_gram[piece] = lax.dot_general(
            mine[0] if len(mine) == 1 else jnp.concatenate(mine, axis=0),
            columns[0 : reach * block],
            (((1,), (1,)), ((), ())),
            preferred_element_type=f32,
        )
        cols = pl.ds(0, reach * block)
        for h in range(low, high):
            gram_own[h, :, cols] = own_gram[piece][
                (h - low) * STEP : (h - low + 1) * STEP
            ].astype(bf16)
        steps_now = pl.ds(low, high - low)
        for k in range(1, fsdp_count):
            send(
                gram_own.at[steps_now, :, cols],
                gram_in.at[k - 1, steps_now, :, cols],
                2,
                gram_wide_sem.at[piece],
                (d, lax.rem(f + k, fsdp_count)),
            )

    def whole_gram(piece):
        low, high, reach = pieces[piece]
        cols = pl.ds(0, reach * block)
        steps_now = pl.ds(low, high - low)
        here = pl.ds(pl.multiple_of(d * STEP, STEP), STEP)
        wait_for(gram_in.at[:, steps_now, :, cols], gram_wide_sem.at[piece])
        for h in range(low, high):
            total = own_gram[piece][(h - low) * STEP : (h - low + 1) * STEP]
            for k in range(1, fsdp_count):
                total = total + gram_in[k - 1, h, :, cols].astype(f32)
            gram[h, here, cols] = total.astype(bf16)
        mine = gram.at[steps_now, here, cols]
        for k in range(1, dp_count):
            send(mine, mine, 3, last_sem.at[0], (lax.rem(d + k, dp_count), f))

    corner = pl.ds((steps - 1) * block, block)
    corner_total = {}
    middle = block // 2
    quarter = block // 4

    def part_corner():
        wait_for(stripes(chips * STEP * width), core_sem.at[steps - 1])
        newest = columns[corner]
        full = lax.dot_general(
            newest, newest, (((1,), (1,)), ((), ())), preferred_element_type=f32
        )
        packed = jnp.concatenate(
            [
                full[middle:block],
                jnp.concatenate([full[0:quarter, 0:middle], full[quarter:middle, 0:middle]], axis=1),
            ],
            axis=0,
        )
        corner_total[0] = packed
        corner_own[...] = packed.astype(bf16)
        for k in range(1, fsdp_count):
            send(
                corner_own,
                corner_in.at[k - 1],
                6,
                last_sem.at[3],
                (d, lax.rem(f + k, fsdp_count)),
            )

    def whole_corner():
        wait_for(corner_in, last_sem.at[3])
        total = corner_total[0]
        for k in range(1, fsdp_count):
            total = total + corner_in[k - 1].astype(f32)
        total = total.astype(bf16).astype(f32)
        first_half = jnp.concatenate(
            [total[middle:, 0:middle], total[middle:, middle:block]], axis=0
        )
        first_half = jnp.concatenate([first_half, jnp.zeros_like(first_half)], axis=1)
        gram[steps - 1, pl.ds(0, middle), corner] = first_half.astype(bf16)
        gram[steps - 1, pl.ds(middle, middle), corner] = total[0:middle].astype(bf16)

    def stats_send():
        total = square_sum[0]
        for value in square_sum[1:]:
            total = total + value
        peaks_copy.wait()
        stats_in[d] = jnp.full((8, 128), total, f32)
        stats_in[d, 0:1, 0:HEADS] = peaks[...].astype(f32)
        for k in range(1, dp_count):
            send(
                stats_in.at[d, pl.ds(0, 2)],
                stats_in.at[d, pl.ds(0, 2)],
                4,
                last_sem.at[1],
                (lax.rem(d + k, dp_count), f),
            )

    def stats_pass():
        wait_for(stats_in.at[pl.ds(0, dp_count - 1), pl.ds(0, 2)], last_sem.at[1])
        stats_wide[f, 0:1] = functools.reduce(
            jnp.maximum, [stats_in[j, 0:1] for j in range(dp_count)]
        )
        stats_wide[f, 1:2] = sum(stats_in[j, 1:2] for j in range(dp_count))
        for k in range(1, fsdp_count):
            send(
                stats_wide.at[f, pl.ds(0, 2)],
                stats_wide.at[f, pl.ds(0, 2)],
                5,
                last_sem.at[2],
                (d, lax.rem(f + k, fsdp_count)),
            )

    def stats_end():
        wait_for(stats_wide.at[pl.ds(0, fsdp_count - 1), pl.ds(0, 2)], last_sem.at[2])
        stats_out[0:1] = functools.reduce(
            jnp.maximum, [stats_wide[j, 0:1] for j in range(fsdp_count)]
        )
        stats_out[1:2] = sum(stats_wide[j, 1:2] for j in range(fsdp_count))

    acts = {
        "F": first_send,
        "S": second_send,
        "B": blend,
        "P": pass_on,
        "D": pass_diagonal,
        "G": part_gram,
        "Z": whole_gram,
        "C": part_corner,
        "E": whole_corner,
        "T": stats_send,
        "U": stats_pass,
    }
    for act in order_of(steps):
        acts[act[0]](*(int(digit) for digit in act[1:]))
    stats_end()
    wait_for(stripes(volume[3]), last_sem.at[0])
    if volume[6]:
        wait_for(corner_in, sent_sem.at[6])
    for sender in range(4):
        if volume[sender]:
            wait_for(stripes(volume[sender]), sent_sem.at[sender])
    wait_for(stats_in.at[pl.ds(0, dp_count - 1), pl.ds(0, 2)], sent_sem.at[4])
    wait_for(stats_wide.at[pl.ds(0, fsdp_count - 1), pl.ds(0, 2)], sent_sem.at[5])


def reduce_and_gather(gradient, momentum, peaks):
    dp_count = lax.axis_size("dp")
    fsdp_count = lax.axis_size("fsdp")
    chips = dp_count // 2
    rows, width = momentum.shape
    steps = rows // STEP
    half = width // 2
    square_plane = chips == 4
    gradient = gradient.reshape(chips, 2, steps, STEP, width)
    in_hbm = pl.BlockSpec(memory_space=pltpu.HBM)
    in_vmem = pl.BlockSpec(memory_space=pltpu.VMEM)
    if square_plane:
        first = (steps, 2, 2, STEP, half)
        second = (steps, 2, STEP, half)
    else:
        first = (steps, chips - 1, STEP, width)
        second = (1, 1, STEP, 128)
    dma = pltpu.SemaphoreType.DMA
    return pl.pallas_call(
        functools.partial(exchange, dp_count, fsdp_count),
        out_shape=(
            pltpu.VMEM((rows, width), f32),
            pltpu.VMEM((KVL, width), bf16),
            pltpu.VMEM((steps, dp_count * STEP, KVL), bf16),
            pltpu.VMEM((8, 128), f32),
        ),
        in_specs=[in_hbm] * 3,
        out_specs=(in_vmem,) * 4,
        scratch_shapes=[
            pltpu.VMEM((steps, chips, STEP, width), bf16),
            pltpu.VMEM((steps, chips, STEP, width), bf16),
            pltpu.VMEM((rows, width), f32),
            pltpu.VMEM((1, HEADS), jnp.int32),
            pltpu.VMEM(first, bf16),
            pltpu.VMEM(first, bf16),
            pltpu.VMEM(second, bf16),
            pltpu.VMEM(second, bf16),
            pltpu.VMEM((steps, STEP, KVL), bf16),
            pltpu.VMEM((fsdp_count - 1, steps, STEP, KVL), bf16),
            pltpu.VMEM((dp_count, 8, 128), f32),
            pltpu.VMEM((fsdp_count, 8, 128), f32),
            dma((steps + 2,)),
            dma((SENDERS,)),
            dma((steps,)),
            dma((steps,)),
            dma((steps,)),
            dma((steps,)),
            dma((steps,)),
            dma((steps,)),
            dma((len(pieces_of(steps)),)),
            dma((4,)),
            pltpu.VMEM((dp_count * STEP * 3 // 4, dp_count * STEP), bf16),
            pltpu.VMEM((fsdp_count - 1, dp_count * STEP * 3 // 4, dp_count * STEP), bf16),
        ],
        compiler_params=pltpu.CompilerParams(
            collective_id=0, has_side_effects=True, vmem_limit_bytes=24 * 1024 * 1024
        ),
        cost_estimate=pl.CostEstimate(
            flops=40_000_000_000, bytes_accessed=4_000_000, transcendentals=0
        ),
    )(*(pltpu.with_memory_space_constraint(x, pltpu.HBM) for x in (gradient, momentum, peaks)))


def product(left, right):
    return jnp.dot(left.astype(bf16), right.astype(bf16), preferred_element_type=f32)


def finish(
    dp_count,
    new_momentum,
    columns,
    gram,
    stats,
    weight,
    clip,
    new_weight_all,
    new_momentum_all,
    update_norm,
    new_weight,
    full_gram,
    small_sem,
    out_sem,
):
    rows, width = new_momentum.shape
    steps = rows // STEP
    span = NOPE + VDIM
    heads = width // span
    lead, second, third = quintic_terms
    momentum_copy = pltpu.make_async_copy(new_momentum, new_momentum_all, small_sem.at[0])
    momentum_copy.start()

    block = dp_count * STEP
    for i in range(steps):
        reach = (i + 1) * block
        full_gram[i * block : reach, 0:reach] = gram[i, :, 0:reach]
        if i and i == steps - 1:
            middle = reach - block // 2
            piece = gram[i, block // 2 : block, i * block : middle].astype(f32)
            full_gram[i * block : middle, middle:reach] = piece.T.astype(bf16)
        for j in range(i):
            piece = gram[i, :, j * block : (j + 1) * block].astype(f32)
            full_gram[j * block : (j + 1) * block, i * block : reach] = piece.T.astype(bf16)

    level = stats[1:2, 0:1]
    update_norm[0] = jnp.sqrt(level * (1.0 / (KVL * KVO)))[0, 0]
    inverse = 1.0 / (jnp.sqrt(level) + epsilon)
    scale = inverse * inverse
    total = full_gram[...]
    gram_now = total.astype(f32) * scale
    square = (scale * scale) * jnp.dot(total, total, preferred_element_type=f32)
    rest = second * gram_now + third * square
    beyond = rest
    part = lead * gram_now + scale * jnp.dot(
        rest.astype(bf16), total, preferred_element_type=f32
    )
    for iteration in range(1, ITERS):
        gram_now = lead * part + product(part, rest)
        rest = second * gram_now + third * product(gram_now, gram_now)
        beyond = lead * beyond + lead**iteration * rest + product(rest, beyond)
        if iteration < ITERS - 1:
            part = lead * gram_now + product(rest, gram_now)
    row = lax.broadcasted_iota(jnp.int32, (KVL, KVL), 0)
    col = lax.broadcasted_iota(jnp.int32, (KVL, KVL), 1)
    whole = jnp.where(row == col, beyond + lead**ITERS, beyond).astype(bf16)

    threshold = clip[0].astype(f32)
    factors = jnp.sqrt(jnp.minimum(1.0, threshold / stats[0:1]))
    lane = lax.broadcasted_iota(jnp.int32, (1, 128), 1)
    first_head = lax.axis_index("fsdp") * heads
    update_scale = (learning_rate * update_gain * math.sqrt(max(KVL, KVO))) * inverse
    factor_row = jnp.concatenate(
        [
            piece
            for j in range(heads)
            for piece in (
                jnp.broadcast_to(
                    jnp.sum(
                        jnp.where(lane == first_head + j, factors, 0.0), axis=1, keepdims=True
                    ),
                    (1, NOPE),
                ),
                jnp.ones((1, VDIM), f32),
            )
        ],
        axis=1,
    )
    keep = factor_row * (1.0 - learning_rate * weight_decay)
    move = factor_row * update_scale
    out_copies = []
    group = min(GROUP, steps)
    for g in range(steps // group):
        rows_now = whole[g * group * block : (g + 1) * group * block]
        for j in range(width // span):
            cols = pl.ds(j * span, span)
            orthogonal = jnp.dot(rows_now, columns[:, cols], preferred_element_type=f32)
            for i in range(group):
                h = g * group + i
                for device in range(dp_count):
                    start = (i * dp_count + device) * STEP
                    new_weight[device, h, :, cols] = (
                        keep[:, j * span : (j + 1) * span] * weight[device, h, :, cols]
                        - move[:, j * span : (j + 1) * span] * orthogonal[start : start + STEP]
                    )
        here = pl.ds(g * group, group)
        copy = pltpu.make_async_copy(
            new_weight.at[:, here], new_weight_all.at[:, here], out_sem.at[g]
        )
        copy.start()
        out_copies.append(copy)
    momentum_copy.wait()
    for copy in out_copies:
        copy.wait()


def polish(new_momentum, columns, gram, stats, weight, clip_threshold):
    dp_count = lax.axis_size("dp")
    rows, width = new_momentum.shape
    steps = rows // STEP
    in_hbm = pl.BlockSpec(memory_space=pltpu.HBM)
    in_vmem = pl.BlockSpec(memory_space=pltpu.VMEM)
    dma = pltpu.SemaphoreType.DMA
    weight = weight.reshape(dp_count, steps, STEP, width)
    new_weight, new_momentum, update_norm = pl.pallas_call(
        functools.partial(finish, dp_count),
        out_shape=(
            jax.ShapeDtypeStruct((dp_count, steps, STEP, width), f32),
            jax.ShapeDtypeStruct((rows, width), f32),
            jax.ShapeDtypeStruct((1,), f32),
        ),
        in_specs=[in_vmem] * 5 + [pl.BlockSpec(memory_space=pltpu.SMEM)],
        out_specs=(in_hbm, in_hbm, pl.BlockSpec(memory_space=pltpu.SMEM)),
        scratch_shapes=[
            pltpu.VMEM((dp_count, steps, STEP, width), f32),
            pltpu.VMEM((KVL, KVL), bf16),
            dma((1,)),
            dma((steps,)),
        ],
        compiler_params=pltpu.CompilerParams(vmem_limit_bytes=24 * 1024 * 1024),
    )(new_momentum, columns, gram, stats, weight, clip_threshold)
    return new_weight.reshape(KVL, width), new_momentum, update_norm


def local(gradients, momentum, weight, logit_peaks, clip_threshold):
    exchanged = reduce_and_gather(gradients, momentum, logit_peaks)
    return polish(*exchanged, weight, clip_threshold)


def solution(mesh):
    placed = (P("dp", None, "fsdp"), P("dp", "fsdp"), P(None, "fsdp"), P(("dp", "fsdp"), None), P())
    return jax.shard_map(
        local,
        mesh=mesh,
        in_specs=placed,
        out_specs=(P(None, "fsdp"), P("dp", "fsdp"), P()),
        check_vma=False,
    )
```
